256 devices in a mesh: row: 16 (over y_hi, x, core), col: 16 (over z, y_lo).
Axes of the slice: x: 4, y: 4 (y_hi: 2, y_lo: 2; y = y_hi * 2 + y_lo), z: 8, core: 2. Of those that a mesh axis runs over, the one named last changes fastest.
Arguments:
- queries: bfloat16 [2048, 3072], P('row'), may hold values from -30 to 30
- latent_pool: bfloat16 [512, 64, 576], P('col'), may hold values from -6 to 6
- block_table: int32 [512], P('col'), may hold values from 0 to 31, as said below
- page_len: int32 [512], P('col'), may hold values from 16 to 64
- group_offset: int32 [1], replicated, may hold values from 0 to 30720
- hidden: bfloat16 [2048, 2048], P('row'), may hold values from -4 to 4
- latent_up: bfloat16 [512, 4096], replicated, may hold values from -0.25 to 0.25
- output_weight: bfloat16 [2048, 2048], P('col'), may hold values from -0.1875 to 0.1875
- gate_weight: bfloat16 [2048, 10944], P('row', 'col'), may hold values from -0.125 to 0.125
- up_weight: bfloat16 [2048, 10944], P('row', 'col'), may hold values from -0.125 to 0.125
- down_weight: bfloat16 [10944, 2048], P('col', 'row'), may hold values from -0.078125 to 0.078125
Outputs:
- attended: bfloat16 [2048, 2048], P('row')
- block_out: bfloat16 [2048, 2048], P('row', 'col')
The draws below stay inside these ranges and needn't reach their ends.
Inputs may be any that keep to these rules, and one draw needn't show every extreme that they name: `block_table`: the 32 logical pages of one col index name its 32 pool pages, each once.
All inputs are finite; a program needn't handle non-finite values.
Results may differ from the reference program's by a relative error of at most 0.015.
Values may be sent and summed in bfloat16 or wider, within the bound.
A program may use at most 128 MiB of HBM per device.

```python
import math
import jax
import jax.numpy as jnp
from jax import lax

D = 2048
H = 16
NOPE = 128
ROPE = 64
VDIM = 128
LATENT = 512
FF = 10944
PAGE = 64
PAGES_DEV = 32
QK = 192
CACHE_W = 576
Q = 2048
L = 32768
NPAGES = 512


def shared_draw(key):
    col_count = NPAGES // PAGES_DEV
    perm_keys = jax.random.split(jax.random.fold_in(key, 11), col_count)
    local_pages = jax.vmap(lambda one_key: jax.random.permutation(one_key, PAGES_DEV))(perm_keys)
    table = local_pages.reshape(NPAGES).astype(jnp.int32)
    pool_values = jnp.clip(jax.random.normal(jax.random.fold_in(key, 12), (NPAGES, PAGE, LATENT + ROPE), jnp.float32), -6.0, 6.0)
    query_values = 2.5 * jnp.clip(jax.random.normal(jax.random.fold_in(key, 13), (Q, H, QK), jnp.float32), -6.0, 6.0)
    strong_rows = jax.random.bernoulli(jax.random.fold_in(key, 20), 0.25, (Q, 1, 1))
    query_values = query_values * jnp.where(strong_rows, 4.0, 1.0)
    query_values = jnp.clip(query_values, -30.0, 30.0)
    return (table, pool_values, query_values.reshape(Q, H * QK))


def draw_queries(key, part):
    return shared_draw(key)[2].astype(jnp.bfloat16)


def draw_latent_pool(key, part):
    return shared_draw(key)[1].astype(jnp.bfloat16)


def draw_block_table(key, part):
    return shared_draw(key)[0]


def draw_page_len(key, part):
    lengths = jax.random.randint(jax.random.fold_in(key, 16), (NPAGES,), PAGE // 4, PAGE + 1).astype(jnp.int32)
    lengths = lengths.at[0].set(PAGE)
    return lengths.at[NPAGES - 1].set(PAGE // 4)


def draw_hidden(key, part):
    values = jnp.clip(jax.random.normal(jax.random.fold_in(key, 17), (Q, D), jnp.float32), -6.0, 6.0)
    trend = 3.0 ** (jnp.arange(D, dtype=jnp.float32) / D)
    col_gain = 0.02 * trend * 10.0 ** jax.random.uniform(jax.random.fold_in(key, 18), (D,), jnp.float32, 0.0, 1.0)
    values = values * col_gain[None, :]
    return values.astype(jnp.bfloat16)


def raised(result, stream_key, source, target, shards_of, factor):
    def block_of(axis_at):
        return (jnp.arange(result.shape[axis_at]) // (result.shape[axis_at] // shards_of)).reshape((-1,) + (1,) * (result.ndim - 1 - axis_at))

    near = jax.random.permutation(stream_key, shards_of)[block_of(target)]
    other_side = (block_of(target) + shards_of // 2) % shards_of
    return jnp.where((block_of(source) == near) | (block_of(source) == other_side), factor * result, result)


def shard_levels(stream_key, shape, pieces, smallest, high):
    level = 1.0
    for position, shards_of in pieces:
        draws = jax.random.uniform(jax.random.fold_in(jax.random.fold_in(stream_key, 6), position), (shards_of,), jnp.float32, smallest / len(pieces), high / len(pieces))
        level = level * jnp.repeat(jnp.exp(draws), shape[position] // shards_of).reshape((-1,) + (1,) * (len(shape) - 1 - position))
    return level


def noise(stream_key, shape, scale, reach, cuts=(), kind=jnp.bfloat16):
    entries = jax.random.normal(stream_key, shape, jnp.float32) * scale
    if len(cuts) > 0:
        entries = shard_levels(stream_key, shape, cuts, -0.22, 0.18) * entries
    return jnp.clip(entries, min=-reach, max=reach).astype(kind)


def heavy_noise(key, extent, spread, bound, shards, heavy, held_as=jnp.bfloat16):
    entries = spread * jax.random.normal(key, extent, jnp.float32)
    if shards:
        entries = entries * shard_levels(key, extent, shards, -0.22, 0.18)
    return jnp.clip(raised(entries, jax.random.fold_in(key, 3), *heavy), -bound, bound).astype(held_as)


def setup_inputs(seed: int = 0) -> dict:
    arg_keys = jax.random.split(jax.random.key(seed), 12)
    queries = draw_queries(jax.random.fold_in(arg_keys[11], 71), 0)
    latent_pool = draw_latent_pool(jax.random.fold_in(arg_keys[11], 71), 0)
    block_table = draw_block_table(jax.random.fold_in(arg_keys[11], 71), 0)
    page_len = draw_page_len(jax.random.fold_in(arg_keys[11], 71), 0)
    group_offset = jax.random.randint(arg_keys[4], (1,), 0, L - Q + 1).astype(jnp.int32)
    hidden = draw_hidden(jax.random.fold_in(arg_keys[11], 71), 0)
    latent_up = noise(arg_keys[6], (LATENT, H * (NOPE + VDIM)), LATENT ** -0.5, 0.25)
    output_weight = heavy_noise(arg_keys[7], (H * VDIM, D), (H * VDIM) ** -0.5, 0.1875, ((0, 16),), (0, 1, 16, 2.0))
    gate_weight = noise(arg_keys[8], (D, FF), D ** -0.5, 0.125, ((0, 16), (1, 16)))
    up_weight = noise(arg_keys[9], (D, FF), D ** -0.5, 0.125, ((0, 16), (1, 16)))
    down_weight = heavy_noise(arg_keys[10], (FF, D), FF ** -0.5, 0.078125, ((0, 16), (1, 16)), (0, 1, 16, 2.0))
    return {"queries": queries, "latent_pool": latent_pool, "block_table": block_table, "page_len": page_len, "group_offset": group_offset, "hidden": hidden, "latent_up": latent_up, "output_weight": output_weight, "gate_weight": gate_weight, "up_weight": up_weight, "down_weight": down_weight}


def reference(queries, latent_pool, block_table, page_len, group_offset, hidden, latent_up, output_weight, gate_weight, up_weight, down_weight):
    owners = jnp.arange(NPAGES, dtype=jnp.int32) // PAGES_DEV * PAGES_DEV
    latent = latent_pool[owners + block_table].reshape(L, CACHE_W)
    key_index = jnp.arange(L, dtype=jnp.int32)
    key_valid = key_index % PAGE < jnp.repeat(page_len, PAGE)
    query_pos = group_offset[0] + jnp.arange(Q, dtype=jnp.int32)
    per_head = queries.reshape(Q, H, QK)
    score_scale = 1.0 / math.sqrt(QK)
    block_rows = math.gcd(Q, 512)

    def one_head(head_index):
        columns = lax.dynamic_slice_in_dim(latent_up, head_index * (NOPE + VDIM), NOPE + VDIM, 1)
        expanded = jnp.dot(latent[:, :LATENT], columns, preferred_element_type=jnp.float32).astype(jnp.bfloat16)
        key_rows = jnp.concatenate([expanded[:, :NOPE], latent[:, LATENT:]], axis=1)
        values = expanded[:, NOPE:]
        head_queries = lax.dynamic_index_in_dim(per_head, head_index, 1, keepdims=False)

        def one_block(block_index):
            block_queries = lax.dynamic_slice_in_dim(head_queries, block_index * block_rows, block_rows, 0)
            block_pos = lax.dynamic_slice_in_dim(query_pos, block_index * block_rows, block_rows, 0)
            scores = jnp.dot(block_queries, key_rows.T, preferred_element_type=jnp.float32) * score_scale
            visible = key_valid[None, :] & (key_index[None, :] <= block_pos[:, None])
            row_max = lax.optimization_barrier(jnp.max(jnp.where(visible, scores, -jnp.inf), axis=1, keepdims=True))
            weights = jnp.where(visible, jnp.exp(scores - row_max), 0.0)
            weighted = jnp.dot(weights.astype(jnp.bfloat16), values, preferred_element_type=jnp.float32)
            return (weighted / lax.optimization_barrier(jnp.sum(weights, axis=1, keepdims=True))).astype(jnp.bfloat16)
        blocks = lax.map(one_block, jnp.arange(Q // block_rows, dtype=jnp.int32))
        return blocks.reshape(Q, VDIM)
    head_outputs = lax.map(one_head, jnp.arange(H, dtype=jnp.int32))
    head_mix = jnp.transpose(head_outputs, (1, 0, 2)).reshape(Q, H * VDIM)
    projected = jnp.dot(head_mix, output_weight, preferred_element_type=jnp.float32)
    attended = (hidden.astype(jnp.float32) + projected).astype(jnp.bfloat16)
    wide = attended.astype(jnp.float32)
    mean_square = lax.optimization_barrier(jnp.mean(wide * wide, axis=1, keepdims=True))
    normed = (wide * lax.rsqrt(mean_square + 1e-06)).astype(jnp.bfloat16)
    gate_sum = jnp.dot(normed, gate_weight, preferred_element_type=jnp.float32)
    up_sum = jnp.dot(normed, up_weight, preferred_element_type=jnp.float32)
    activated = (jax.nn.silu(gate_sum) * up_sum).astype(jnp.bfloat16)
    mlp_terms = jnp.dot(activated, down_weight, preferred_element_type=jnp.float32)
    block_out = (wide + mlp_terms).astype(jnp.bfloat16)
    return (attended, block_out)
```

```python
import functools
import math

import jax
import jax.numpy as jnp
from jax import lax
from jax.experimental import pallas as pl
from jax.experimental.pallas import tpu as pltpu
from jax.sharding import PartitionSpec as P

H = 16
NOPE = 128
ROPE = 64
VDIM = 128
LATENT = 512
QK = 192
MESH = pl.DeviceIdType.MESH
LOW = -1e30
FAR = 1 << 30
SCALE2 = math.log2(math.e) / math.sqrt(QK)
F32 = jnp.float32
BF16 = jnp.bfloat16
YP, XP, XM, SIB, DN = range(5)
KEY_CHUNK = 256


def dot(a, b):
    return jnp.dot(a, b, preferred_element_type=F32)


def dot_nt(a, b):
    return lax.dot_general(a, b, (((1,), (1,)), ((), ())), preferred_element_type=F32)


def kernel(
    ncol, nx,
    q_h, pool_h, table_s, plen_s, off_s, hid_h, lup_h, wo_h, g_h, u_h, d_h,
    att_o, blk_o,
    lat, lupv, qv, hid, wo, gv, uv, dv, keys, vals, sc, kpos,
    o_send, o_recv, st_send, st_recv, p1_send, p1_recv, att, p2_send, p2_recv, act, blk,
    lsem, lup_sem, own_sem, out_sem, ws_sem, wr_sem,
    o_ss, o_rs, st_ss, st_rs, p1_ss, p1_rs, at_ss, at_rs, p2_ss, p2_rs,
):
    row, col = lax.axis_index("row"), lax.axis_index("col")

    def rem(a, b):
        return a % b

    def div(a, b):
        return a // b

    core, x, yhi = rem(row, 2), rem(div(row, 2), nx), div(row, 2 * nx)

    def row_of(yy, xx, cc):
        return (yy * nx + xx) * 2 + cc

    xp, xm, x2 = rem(x + 1, nx), rem(x + nx - 1, nx), rem(x + 2, nx)
    yo, co = 1 - yhi, 1 - core
    plus = [xp, xm, jnp.where(core == 0, xp, xm)]
    minus = [xm, xp, jnp.where(core == 0, xm, xp)]
    peers = [row_of(yo, x, core), row_of(yhi, xp, core), row_of(yhi, xm, core), row_of(yhi, x, co)]
    ups = [[row_of(yy, minus[t], core) for t in range(3)] for yy in (yhi, yo)]
    dns = [[row_of(yy, plus[t], core) for t in range(3)] for yy in (yhi, yo)]
    x2s = [row_of(yy, x2, core) for yy in (yhi, yo)]
    full = [gv, uv, dv]
    mine_h = [g_h, u_h, d_h]

    pairs = H // 2
    first_pair = div(col, 2) + 1
    loads = [
        pltpu.make_async_copy(pool_h, lat, lsem.at[0]),
        pltpu.make_async_copy(q_h, qv, lsem.at[1]),
        pltpu.make_async_copy(wo_h, wo, lsem.at[2]),
        pltpu.make_async_copy(hid_h.at[:, pl.ds(pl.multiple_of(col * 128, 128), 128)], hid, lsem.at[3]),
    ]

    def lup_load(i):
        p = rem(first_pair + i, pairs)
        return pltpu.make_async_copy(
            lup_h.at[:, pl.ds(pl.multiple_of(p * 512, 512), 512)], lupv.at[p], lup_sem.at[i]
        )

    loads[0].start()
    lup_load(0).start()
    loads[1].start()

    barrier = pltpu.get_barrier_semaphore()

    @pl.loop(1, ncol)
    def _(t):
        pl.semaphore_signal(barrier, inc=1, device_id=(row, rem(col + t, ncol)), device_id_type=MESH)

    for peer in peers:
        pl.semaphore_signal(barrier, inc=1, device_id=(peer, col), device_id_type=MESH)

    for i in range(1, pairs):
        lup_load(i).start()
    own_loads = [pltpu.make_async_copy(mine_h[t], full[t].at[row], own_sem.at[t]) for t in range(3)]
    loads[2].start()
    loads[3].start()
    for c in own_loads:
        c.start()

    base = col * kpos.shape[1]
    lane = lax.broadcasted_iota(jnp.int32, kpos.shape, 1)
    page, slot = lax.shift_right_logical(lane, 6), lane & 63
    kp = jnp.full(kpos.shape, FAR, jnp.int32)
    for p in range(lat.shape[0]):
        here = jnp.where(slot < plen_s[p], base + p * 64 + slot, FAR)
        kp = jnp.where(page == table_s[p], here, kp)
    kpos[...] = kp
    qpos = off_s[0] + row * 128 + lax.broadcasted_iota(jnp.int32, (128, 1), 0)

    pl.semaphore_wait(barrier, ncol - 1 + len(peers))

    sent = []

    def wcopy(t, owner, kind, dest, source=None):
        return pltpu.make_async_remote_copy(
            src_ref=full[t].at[owner] if source is None else source,
            dst_ref=full[t].at[owner],
            send_sem=ws_sem.at[t, kind, owner],
            recv_sem=wr_sem.at[t, owner],
            device_id=(dest, col),
            device_id_type=MESH,
        )

    def wsend(t, owner, kind, dest, source=None):
        wcopy(t, owner, kind, dest, source).start()
        sent.append((t, owner, kind, dest, source))

    def warrive(t, owner):
        wcopy(t, owner, SIB, peers[SIB]).wait_recv()

    def stage_own(t):
        for kind in range(4):
            wsend(t, row, kind, peers[kind], mine_h[t])

    def stage_y(t):
        o = peers[YP]
        warrive(t, o)
        for kind in (XP, XM, SIB):
            wsend(t, o, kind, peers[kind])

    def stage_x(t, yy):
        up, dn = ups[yy][t], dns[yy][t]
        warrive(t, up)
        wsend(t, up, DN, dns[0][t])
        wsend(t, up, SIB, peers[SIB])
        warrive(t, dn)
        wsend(t, dn, SIB, peers[SIB])

    def stage_x2(t, yy):
        o = x2s[yy]
        warrive(t, o)
        wsend(t, o, SIB, peers[SIB])

    def stage_sib(t):
        for yy in range(2):
            for xx in range(nx):
                warrive(t, row_of(yy, xx, co))

    stage_own(0)
    stage_own(1)

    schedule = {
        3: [lambda: stage_x(0, 0), lambda: stage_x(1, 0)],
        5: [lambda: stage_y(0), lambda: stage_y(1), lambda: stage_own(2)],
    }

    loads[0].wait()
    zeros64 = jnp.zeros((keys.shape[1], 64), BF16)
    rope = lat[:, :, LATENT:].reshape(keys.shape[1], ROPE)
    for hh in range(2):
        keys[hh, :, NOPE:] = jnp.concatenate([rope, zeros64], axis=1)
    loads[1].wait()
    nkeys = keys.shape[1]

    def o_copy(head):
        return (
            pltpu.make_async_remote_copy(
                src_ref=o_send.at[head], dst_ref=o_recv.at[col], send_sem=o_ss.at[head],
                recv_sem=o_rs.at[col], device_id=(row, head), device_id_type=MESH),
            pltpu.make_async_remote_copy(
                src_ref=st_send.at[head], dst_ref=st_recv.at[col], send_sem=st_ss.at[head],
                recv_sem=st_rs.at[col], device_id=(row, head), device_id_type=MESH),
        )

    lane128 = lax.broadcasted_iota(jnp.int32, (128, 128), 1)

    @pl.loop(0, pairs)
    def _(i):
        p = rem(first_pair + i, pairs)
        pltpu.make_async_copy(lup_h.at[:, pl.ds(0, 512)], lupv.at[p], lup_sem.at[i]).wait()
        w = lupv[p]
        for kc in range(4):
            rows = slice(kc * 512, (kc + 1) * 512)
            e = dot(lat[kc * 8:(kc + 1) * 8, :, :LATENT].reshape(512, LATENT), w).astype(BF16)
            keys[0, rows, :NOPE] = e[:, :128]
            vals[0, rows, :] = e[:, 128:256]
            keys[1, rows, :NOPE] = e[:, 256:384]
            vals[1, rows, :] = e[:, 384:]
        qp = qv[:, pl.ds(pl.multiple_of(p * 2 * QK, 2 * QK), 2 * QK)]
        zq = jnp.zeros((128, 64), BF16)
        for hh in range(2):
            q = jnp.concatenate([qp[:, hh * QK:(hh + 1) * QK], zq], axis=1)
            best = jnp.full((128, 128), LOW, F32)
            for kc in range(nkeys // KEY_CHUNK):
                ks = slice(kc * KEY_CHUNK, (kc + 1) * KEY_CHUNK)
                s = dot_nt(q, keys[hh, ks, :])
                s = jnp.where(kpos[:, ks] <= qpos, s, LOW)
                sc[hh, :, ks] = s
                for j in range(KEY_CHUNK // 128):
                    best = jnp.maximum(best, s[:, j * 128:(j + 1) * 128])
            m = jnp.max(best, axis=1, keepdims=True)
            mc = jnp.where(m < 0.1 * LOW, 0.0, m) * SCALE2
            tot = jnp.zeros((128, 128), F32)
            out = jnp.zeros((128, 128), F32)
            for kc in range(nkeys // KEY_CHUNK):
                ks = slice(kc * KEY_CHUNK, (kc + 1) * KEY_CHUNK)
                pr = jnp.exp2(sc[hh, :, ks] * SCALE2 - mc)
                for j in range(KEY_CHUNK // 128):
                    tot = tot + pr[:, j * 128:(j + 1) * 128]
                out = out + dot(pr.astype(BF16), vals[hh, ks, :])
            total = jnp.sum(tot, axis=1, keepdims=True)
            stats = jnp.where(lane128 == 0, m * SCALE2, jnp.where(lane128 == 1, total, 0.0))
            st = stats.T[:8, :]
            ob = out.astype(BF16)
            head = p * 2 + hh
            o_send[head] = ob
            st_send[head] = st

            @pl.when(head != col)
            def _():
                for c in o_copy(head):
                    c.start()

            @pl.when(head == col)
            def _():
                o_recv[col] = ob
                st_recv[col] = st

        for at, acts in schedule.items():
            @pl.when(i == at)
            def _():
                for a in acts:
                    a()

    @pl.loop(1, ncol)
    def _(t):
        s = rem(col + t, ncol)
        pltpu.make_async_remote_copy(
            src_ref=o_send.at[s], dst_ref=o_recv.at[s], send_sem=o_ss.at[s], recv_sem=o_rs.at[s],
            device_id=(row, s), device_id_type=MESH).wait_recv()
        pltpu.make_async_remote_copy(
            src_ref=st_send.at[s], dst_ref=st_recv.at[s], send_sem=st_ss.at[s], recv_sem=st_rs.at[s],
            device_id=(row, s), device_id_type=MESH).wait_recv()

    ms, ls = st_recv[:, 0, :], st_recv[:, 1, :]
    top = jnp.max(ms, axis=0, keepdims=True)
    wgt = jnp.exp2(ms - top)
    share = wgt / jnp.sum(wgt * ls, axis=0, keepdims=True)
    share = jnp.concatenate([share, jnp.zeros((128 - ncol, 128), F32)], axis=0).T
    mix = jnp.zeros((128, 128), F32)
    for s in range(ncol):
        mix = mix + share[:, s:s + 1] * o_recv[s].astype(F32)
    mix = mix.astype(BF16)

    def slot_copy(send, recv, ss, rs, dest):
        return pltpu.make_async_remote_copy(
            src_ref=send.at[dest], dst_ref=recv.at[col], send_sem=ss.at[dest], recv_sem=rs.at[col],
            device_id=(row, dest), device_id_type=MESH)

    def arrive(send, recv, ss, rs):
        @pl.loop(1, ncol)
        def _(t):
            s = rem(col + t, ncol)
            pltpu.make_async_remote_copy(
                src_ref=send.at[s], dst_ref=recv.at[s], send_sem=ss.at[s], recv_sem=rs.at[s],
                device_id=(row, s), device_id_type=MESH).wait_recv()

    def spread(term, send, recv, ss, rs, dest):
        send[dest] = term

        @pl.when(dest != col)
        def _():
            slot_copy(send, recv, ss, rs, dest).start()

        @pl.when(dest == col)
        def _():
            recv[col] = term

    loads[2].wait()
    loads[3].wait()

    @pl.loop(0, pairs)
    def _(i):
        p = rem(first_pair + i, pairs)
        term = dot(mix, wo[:, pl.ds(pl.multiple_of(p * 256, 256), 256)]).astype(BF16)
        for hh in range(2):
            spread(term[:, hh * 128:(hh + 1) * 128], p1_send, p1_recv, p1_ss, p1_rs, p * 2 + hh)

    for t in range(2):
        stage_x(t, 1)
    arrive(p1_send, p1_recv, p1_ss, p1_rs)
    acc = hid[...].astype(F32)
    for s in range(ncol):
        acc = acc + p1_recv[s].astype(F32)
    att_mine = acc.astype(BF16)
    att[col] = att_mine

    def att_copy(dest):
        return pltpu.make_async_remote_copy(
            src_ref=att.at[col], dst_ref=att.at[col], send_sem=at_ss.at[dest], recv_sem=at_rs.at[col],
            device_id=(row, dest), device_id_type=MESH)

    @pl.loop(1, ncol)
    def _(t):
        att_copy(rem(col + t, ncol)).start()

    for t in range(2):
        stage_x2(t, 0)
    stage_x(2, 0)
    for t in range(2):
        stage_x2(t, 1)
    stage_y(2)

    @pl.loop(1, ncol)
    def _(t):
        s = rem(col + t, ncol)
        pltpu.make_async_remote_copy(
            src_ref=att.at[s], dst_ref=att.at[s], send_sem=at_ss.at[s], recv_sem=at_rs.at[s],
            device_id=(row, s), device_id_type=MESH).wait_recv()

    att_outs = [pltpu.make_async_copy(att.at[s], att_o.at[:, s * 128:(s + 1) * 128], out_sem.at[s])
                for s in range(ncol)]
    for c in att_outs:
        c.start()

    for c in own_loads:
        c.wait()
    sq = jnp.zeros((128, 128), F32)
    for s in range(ncol):
        a = att[s].astype(F32)
        sq = sq + a * a
    scale = lax.rsqrt(jnp.sum(sq, axis=1, keepdims=True) * (1.0 / (128 * ncol)) + 1e-06)
    for t in range(2):
        stage_sib(t)
    ff = gv.shape[2]
    gate = jnp.zeros((128, ff), F32)
    up = jnp.zeros((128, ff), F32)
    for s in range(0, ncol, 2):
        a = jnp.concatenate([att[s], att[s + 1]], axis=1).astype(F32)
        n = (a * scale).astype(BF16)
        gate = gate + dot(n, gv[s:s + 2].reshape(256, ff))
        up = up + dot(n, uv[s:s + 2].reshape(256, ff))
    act[...] = (gate / (1.0 + jnp.exp(-gate)) * up).astype(BF16)

    stage_x(2, 1)
    stage_x2(2, 0)
    stage_x2(2, 1)
    stage_sib(2)

    @pl.loop(0, pairs)
    def _(i):
        p = rem(first_pair + i, pairs)
        w = jnp.concatenate([dv[2 * p], dv[2 * p + 1]], axis=1)
        term = dot(act[...], w).astype(BF16)
        for hh in range(2):
            spread(term[:, hh * 128:(hh + 1) * 128], p2_send, p2_recv, p2_ss, p2_rs, p * 2 + hh)

    arrive(p2_send, p2_recv, p2_ss, p2_rs)
    acc = att[col].astype(F32)
    for s in range(ncol):
        acc = acc + p2_recv[s].astype(F32)
    blk[...] = acc.astype(BF16)
    blk_out = pltpu.make_async_copy(blk, blk_o, out_sem.at[ncol])
    blk_out.start()

    for t, owner, kind, dest, source in sent:
        wcopy(t, owner, kind, dest, source).wait_send()

    @pl.loop(1, ncol)
    def _(t):
        d = rem(col + t, ncol)
        for c in o_copy(d):
            c.wait_send()
        slot_copy(p1_send, p1_recv, p1_ss, p1_rs, d).wait_send()
        slot_copy(p2_send, p2_recv, p2_ss, p2_rs, d).wait_send()
        att_copy(d).wait_send()

    for c in att_outs:
        c.wait()
    blk_out.wait()


def solution(mesh):
    ncol, nrow = mesh.shape["col"], mesh.shape["row"]
    nx = nrow // 4
    placed = (
        P("row", None), P("col", None, None), P("col"), P("col"), P(), P("row", None), P(),
        P("col", None), P("row", "col"), P("row", "col"), P("col", "row"),
    )

    def on_device(queries, pool, table, plen, off, hidden, lup, wo, gate, up, down):
        rows, d = hidden.shape
        ff = gate.shape[1]
        nkeys = pool.shape[0] * pool.shape[1]
        dma, vm = pltpu.SemaphoreType.DMA, pltpu.VMEM
        anyspec = pl.BlockSpec(memory_space=pl.ANY)
        smem = pl.BlockSpec(memory_space=pltpu.SMEM)
        blocks = (ncol, rows, 128)
        scratch = [
            vm(pool.shape, BF16), vm((H // 2, LATENT, 512), BF16), vm(queries.shape, BF16),
            vm((rows, 128), BF16), vm(wo.shape, BF16),
            vm((nrow,) + gate.shape, BF16), vm((nrow,) + up.shape, BF16), vm((nrow,) + down.shape, BF16),
            vm((2, nkeys, 256), BF16), vm((2, nkeys, VDIM), BF16), vm((2, rows, nkeys), F32),
            vm((1, nkeys), jnp.int32),
            vm(blocks, BF16), vm(blocks, BF16), vm((ncol, 8, 128), F32), vm((ncol, 8, 128), F32),
            vm(blocks, BF16), vm(blocks, BF16), vm(blocks, BF16), vm(blocks, BF16), vm(blocks, BF16),
            vm((rows, ff), BF16), vm((rows, 128), BF16),
            dma((4,)), dma((H // 2,)), dma((3,)), dma((ncol + 1,)), dma((3, 5, nrow)), dma((3, nrow)),
        ] + [dma((ncol,))] * 10
        return pl.pallas_call(
            functools.partial(kernel, ncol, nx),
            out_shape=(
                jax.ShapeDtypeStruct((rows, d), BF16),
                jax.ShapeDtypeStruct((rows, d // ncol), BF16),
            ),
            in_specs=[anyspec, anyspec, smem, smem, smem] + [anyspec] * 6,
            out_specs=(anyspec, anyspec),
            scratch_shapes=scratch,
            compiler_params=pltpu.CompilerParams(
                collective_id=0, has_side_effects=True, vmem_limit_bytes=60 << 20),
            name="block",
        )(queries, pool, table, plen, off, hidden, lup, wo, gate, up, down)

    return jax.shard_map(
        on_device, mesh=mesh, in_specs=placed,
        out_specs=(P("row", None), P("row", "col")), check_vma=False,
    )
```

```python
import functools
import math

import jax
import jax.numpy as jnp
from jax import lax
from jax.experimental import pallas as pl
from jax.experimental.pallas import tpu as pltpu
from jax.sharding import PartitionSpec as P

H = 16
NOPE = 128
ROPE = 64
VDIM = 128
LATENT = 512
QK = 192
MESH = pl.DeviceIdType.MESH
LOW = -1e30
FAR = 1 << 30
SCALE2 = math.log2(math.e) / math.sqrt(QK)
F32 = jnp.float32
BF16 = jnp.bfloat16
YP, XP, XM, SIB, DN = range(5)
KEY_CHUNK = 256
EXPAND = 512
EARLY, LATE = (0,), (0, 3, 6)
FAR_FIRST = (4, 3, 5, 2, 6, 1, 7)
NEAR_FIRST = (1, 7, 2, 6, 3, 5, 4)


def dot(a, b):
    return jnp.dot(a, b, preferred_element_type=F32)


def dot_nt(a, b):
    return lax.dot_general(a, b, (((1,), (1,)), ((), ())), preferred_element_type=F32)


def kernel(
    ncol, nx,
    q_h, pool_h, table_s, plen_s, off_s, hid_h, lup_h, wo_h, g_h, u_h, d_h,
    att_o, blk_o,
    lat, lupv, q2, hid, wo, gv, uv, dv, keys0, keys1, vals0, vals1, sc0, sc1, kpos,
    o_send, o_recv, st_send, st_recv, own_term, y1_send, y1_recv, z1_send, z1_recv, att,
    y2_send, y2_recv, z2_send, z2_recv, act, blk,
    lsem, lup_sem, q_sem, own_sem, out_sem, ws_sem, wr_sem, qs_sem, qr_sem,
    o_ss, o_rs, st_ss, st_rs, y1_ss, y1_rs, z1_ss, z1_rs, at_ss, at_rs, y2_ss, y2_rs, z2_ss, z2_rs,
):
    row, col = lax.axis_index("row"), lax.axis_index("col")

    def rem(a, b):
        return a % b

    def div(a, b):
        return a // b

    core, x, yhi = rem(row, 2), rem(div(row, 2), nx), div(row, 2 * nx)

    def row_of(yy, xx, cc):
        return (yy * nx + xx) * 2 + cc

    xp, xm, x2 = rem(x + 1, nx), rem(x + nx - 1, nx), rem(x + 2, nx)
    yo, co = 1 - yhi, 1 - core
    plus = [xp, xm, jnp.where(core == 0, xp, xm)]
    minus = [xm, xp, jnp.where(core == 0, xm, xp)]
    peers = [row_of(yo, x, core), row_of(yhi, xp, core), row_of(yhi, xm, core), row_of(yhi, x, co)]
    ups = [[row_of(yy, minus[t], core) for t in range(3)] for yy in (yhi, yo)]
    dns = [[row_of(yy, plus[t], core) for t in range(3)] for yy in (yhi, yo)]
    x2s = [row_of(yy, x2, core) for yy in (yhi, yo)]
    full = [gv, uv, dv]
    mine_h = [g_h, u_h, d_h]

    nz = ncol // 2
    z, ylo = div(col, 2), rem(col, 2)
    ynb = z * 2 + 1 - ylo
    sib = peers[SIB]
    steps = nz // 2
    turn = rem(core + z, 2)
    pair_at = [rem(z + 2 + 2 * i + turn, nz) for i in range(steps)]
    other_at = [rem(z + 2 + 2 * i + 1 - turn, nz) for i in range(steps)]

    loads = [
        pltpu.make_async_copy(pool_h, lat, lsem.at[0]),
        pltpu.make_async_copy(wo_h, wo, lsem.at[1]),
        pltpu.make_async_copy(hid_h.at[:, pl.ds(pl.multiple_of(col * 128, 128), 128)], hid, lsem.at[2]),
    ]

    def q_cols(p):
        return q_h.at[:, pl.ds(pl.multiple_of(p * 2 * QK, 2 * QK), 2 * QK)]

    lup_loads = [
        pltpu.make_async_copy(
            lup_h.at[:, pl.ds(pl.multiple_of(pair_at[i] * 512, 512), 512)], lupv.at[i], lup_sem.at[i])
        for i in range(steps)
    ]
    q_loads = [
        pltpu.make_async_copy(q_cols(pair_at[i]), q2.at[i, pl.ds(0, 128), :], q_sem.at[i])
        for i in range(steps)
    ]
    q_sends = [
        pltpu.make_async_remote_copy(
            src_ref=q_cols(other_at[i]), dst_ref=q2.at[i, pl.ds(128, 128), :],
            send_sem=qs_sem.at[i], recv_sem=qr_sem.at[i], device_id=(sib, col), device_id_type=MESH)
        for i in range(steps)
    ]
    lup_loads[0].start()
    loads[0].start()

    barrier = pltpu.get_barrier_semaphore()

    @pl.loop(1, ncol)
    def _(t):
        pl.semaphore_signal(barrier, inc=1, device_id=(row, rem(col + t, ncol)), device_id_type=MESH)

    @pl.loop(0, ncol)
    def _(t):
        pl.semaphore_signal(barrier, inc=1, device_id=(sib, rem(col + t, ncol)), device_id_type=MESH)

    for peer in peers[:SIB]:
        pl.semaphore_signal(barrier, inc=1, device_id=(peer, col), device_id_type=MESH)

    for c in q_loads + lup_loads[1:]:
        c.start()
    own_loads = [pltpu.make_async_copy(mine_h[t], full[t].at[row], own_sem.at[t]) for t in range(3)]
    for c in loads[1:] + own_loads:
        c.start()

    base = col * kpos.shape[1]
    lane = lax.broadcasted_iota(jnp.int32, kpos.shape, 1)
    page, slot = lax.shift_right_logical(lane, 6), lane & 63
    kp = jnp.full(kpos.shape, FAR, jnp.int32)
    for p in range(lat.shape[0]):
        here = jnp.where(slot < plen_s[p], base + p * 64 + slot, FAR)
        kp = jnp.where(page == table_s[p], here, kp)
    kpos[...] = kp
    sub = lax.broadcasted_iota(jnp.int32, (256, 1), 0)
    qpos = off_s[0] + jnp.where(sub < 128, row * 128 + sub, sib * 128 + sub - 128)

    nkeys = keys0.shape[1]
    bufs = [(keys0, vals0), (keys1, vals1)]

    def expand(i, kc, size):
        keys, vals = bufs[i % 2]
        rows = slice(kc * size, (kc + 1) * size)
        pages = slice(kc * size // 64, (kc + 1) * size // 64)
        e = dot(lat[pages, :, :LATENT].reshape(size, LATENT), lupv[i]).astype(BF16)
        keys[0, rows, :NOPE] = e[:, :128]
        vals[0, rows, :] = e[:, 128:256]
        keys[1, rows, :NOPE] = e[:, 256:384]
        vals[1, rows, :] = e[:, 384:]

    loads[0].wait()
    zeros64 = jnp.zeros((nkeys, 64), BF16)
    rope = jnp.concatenate([lat[:, :, LATENT:].reshape(nkeys, ROPE), zeros64], axis=1)
    for keys, _v in bufs:
        for hh in range(2):
            keys[hh, :, NOPE:] = rope
    lup_loads[0].wait()
    for kc in range(nkeys // EXPAND):
        expand(0, kc, EXPAND)

    pl.semaphore_wait(barrier, 2 * ncol - 1 + len(peers) - 1)
    for c in q_sends:
        c.start()

    sent = []

    def wcopy(t, owner, kind, dest, source=None):
        return pltpu.make_async_remote_copy(
            src_ref=full[t].at[owner] if source is None else source,
            dst_ref=full[t].at[owner],
            send_sem=ws_sem.at[t, kind, owner],
            recv_sem=wr_sem.at[t, owner],
            device_id=(dest, col),
            device_id_type=MESH,
        )

    def wsend(t, owner, kind, dest, source=None):
        wcopy(t, owner, kind, dest, source).start()
        sent.append((t, owner, kind, dest, source))

    def warrive(t, owner):
        wcopy(t, owner, SIB, sib).wait_recv()

    def stage_own(t):
        for kind in range(4):
            wsend(t, row, kind, peers[kind], mine_h[t])

    def stage_y(t):
        o = peers[YP]
        warrive(t, o)
        for kind in (XP, XM, SIB):
            wsend(t, o, kind, peers[kind])

    def stage_x(t, yy):
        up, dn = ups[yy][t], dns[yy][t]
        warrive(t, up)
        wsend(t, up, DN, dns[0][t])
        wsend(t, up, SIB, sib)
        warrive(t, dn)
        wsend(t, dn, SIB, sib)

    def stage_x2(t, yy):
        o = x2s[yy]
        warrive(t, o)
        wsend(t, o, SIB, sib)

    def stage_sib(t):
        for yy in range(2):
            for xx in range(nx):
                warrive(t, row_of(yy, xx, co))

    plan = {
        "start": [(stage_own, 0), (stage_own, 1)],
        1: [(stage_x, 0, 0), (stage_x, 1, 0), (stage_own, 2)],
        3: [(stage_y, 0), (stage_y, 1)],
        "proj_z": [(stage_x, 2, 0), (stage_y, 2)],
        "gather": [(stage_x, 0, 1), (stage_x, 1, 1), (stage_x2, 0, 0), (stage_x2, 1, 0)],
        "gather_y": [(stage_x2, 0, 1), (stage_x2, 1, 1), (stage_x, 2, 1), (stage_x2, 2, 0)],
        "gateup": [(stage_sib, 0), (stage_sib, 1)],
        "down": [(stage_x2, 2, 1), (stage_sib, 2)],
    }

    def at_point(name):
        for stage, *which in plan.get(name, ()):
            stage(*which)

    at_point("start")

    def o_copies(part, head):
        dest = sib if part else row
        return (
            pltpu.make_async_remote_copy(
                src_ref=o_send.at[part, head], dst_ref=o_recv.at[col], send_sem=o_ss.at[part, head],
                recv_sem=o_rs.at[col], device_id=(dest, head), device_id_type=MESH),
            pltpu.make_async_remote_copy(
                src_ref=st_send.at[part, head], dst_ref=st_recv.at[col], send_sem=st_ss.at[part, head],
                recv_sem=st_rs.at[col], device_id=(dest, head), device_id_type=MESH),
        )

    lane128 = lax.broadcasted_iota(jnp.int32, (128, 128), 1)
    scs = [sc0, sc1]
    nchunk = nkeys // KEY_CHUNK
    mine = rem(div(col, 2) + core, 2) == 0
    for i in range(steps):
        keys, vals = bufs[i % 2]
        more = i + 1 < steps
        q_loads[i].wait()
        q_sends[i].wait_recv()
        if more:
            lup_loads[i + 1].wait()
        zq = jnp.zeros((256, 64), BF16)
        qs = [jnp.concatenate([q2[i, :, hh * QK:(hh + 1) * QK], zq], axis=1) for hh in range(2)]
        best = [jnp.full((256, 128), LOW, F32)] * 2
        for kc in range(nchunk):
            ks = slice(kc * KEY_CHUNK, (kc + 1) * KEY_CHUNK)
            if more and kc in EARLY:
                expand(i + 1, EARLY.index(kc), EXPAND)
            for hh in range(2):
                s = dot_nt(qs[hh], keys[hh, ks, :])
                s = jnp.where(kpos[:, ks] <= qpos, s, LOW)
                scs[hh][:, ks] = s
                for j in range(KEY_CHUNK // 128):
                    best[hh] = jnp.maximum(best[hh], s[:, j * 128:(j + 1) * 128])
        ms = [jnp.max(b, axis=1, keepdims=True) for b in best]
        mc = [jnp.where(m < 0.1 * LOW, 0.0, m) * SCALE2 for m in ms]
        tot = [jnp.zeros((256, 128), F32)] * 2
        out = [jnp.zeros((256, 128), F32)] * 2
        for kc in range(nchunk):
            ks = slice(kc * KEY_CHUNK, (kc + 1) * KEY_CHUNK)
            if more and kc in LATE:
                expand(i + 1, len(EARLY) + LATE.index(kc), EXPAND)
            for hh in range(2):
                pr = jnp.exp2(scs[hh][:, ks] * SCALE2 - mc[hh])
                for j in range(KEY_CHUNK // 128):
                    tot[hh] = tot[hh] + pr[:, j * 128:(j + 1) * 128]
                out[hh] = out[hh] + dot(pr.astype(BF16), vals[hh, ks, :])
        for hh in range(2):
            head = pair_at[i] * 2 + hh
            total = jnp.sum(tot[hh], axis=1, keepdims=True)
            for part in range(2):
                rs = slice(part * 128, (part + 1) * 128)
                stats = jnp.where(lane128 == 0, ms[hh][rs] * SCALE2, jnp.where(lane128 == 1, total[rs], 0.0))
                o_send[part, head] = out[hh][rs].astype(BF16)
                st_send[part, head] = stats.T[:8, :]
        for hh in range(2):
            head = pair_at[i] * 2 + hh
            for c in o_copies(1, head):
                c.start()

            @pl.when(head != col)
            def _():
                for c in o_copies(0, head):
                    c.start()

            @pl.when(head == col)
            def _():
                o_recv[col] = o_send[0, col]
                st_recv[col] = st_send[0, col]

        at_point(i)

    def o_arrive(s):
        pltpu.make_async_remote_copy(
            src_ref=o_send.at[0, s], dst_ref=o_recv.at[s], send_sem=o_ss.at[0, s], recv_sem=o_rs.at[s],
            device_id=(sib, s), device_id_type=MESH).wait_recv()
        pltpu.make_async_remote_copy(
            src_ref=st_send.at[0, s], dst_ref=st_recv.at[s], send_sem=st_ss.at[0, s], recv_sem=st_rs.at[s],
            device_id=(sib, s), device_id_type=MESH).wait_recv()

    @pl.loop(1, ncol)
    def _(t):
        o_arrive(rem(col + t, ncol))

    @pl.when(jnp.logical_not(mine))
    def _():
        o_arrive(col)

    ms, ls = st_recv[:, 0, :], st_recv[:, 1, :]
    top = jnp.max(ms, axis=0, keepdims=True)
    wgt = jnp.exp2(ms - top)
    share = wgt / jnp.sum(wgt * ls, axis=0, keepdims=True)
    share = jnp.concatenate([share, jnp.zeros((128 - ncol, 128), F32)], axis=0).T
    mix = jnp.zeros((128, 128), F32)
    for s in range(ncol):
        mix = mix + share[:, s:s + 1] * o_recv[s].astype(F32)
    mix = mix.astype(BF16)

    def rcopy(src, dst, ss, rs, dest):
        return pltpu.make_async_remote_copy(
            src_ref=src, dst_ref=dst, send_sem=ss, recv_sem=rs, device_id=(row, dest), device_id_type=MESH)

    def y_copy(bufs5, zz):
        ys, yr, yss, yrs = bufs5[:4]
        return rcopy(ys.at[zz], yr.at[zz], yss.at[zz], yrs.at[zz], ynb)

    def z_copy(bufs5, zz, mine_slot):
        zs, zr, zss, zrs = bufs5[4:]
        return rcopy(zs.at[zz], zr.at[mine_slot], zss.at[zz], zrs.at[mine_slot], zz * 2 + ylo)

    def sum_over_col(term_of, start, bufs5, name):
        for off in FAR_FIRST + (0,):
            zz = rem(z + off, nz)
            both = term_of(zz)
            a, b = both[:, :128], both[:, 128:]
            own_term[zz] = jnp.where(ylo == 0, a, b)
            bufs5[0][zz] = jnp.where(ylo == 0, b, a).astype(BF16)
            y_copy(bufs5, zz).start()
        at_point(name + "_y")
        acc = start
        for off in FAR_FIRST + (0,):
            zz = rem(z + off, nz)
            y_copy(bufs5, zz).wait_recv()
            pair = own_term[zz] + bufs5[1][zz].astype(F32)
            if off:
                bufs5[4][zz] = pair.astype(BF16)
                z_copy(bufs5, zz, z).start()
            else:
                acc = acc + pair
        at_point(name + "_z")
        for off in NEAR_FIRST:
            zz = rem(z + off, nz)
            z_copy(bufs5, zz, zz).wait_recv()
            acc = acc + bufs5[5][zz].astype(F32)
        return acc

    set1 = (y1_send, y1_recv, y1_ss, y1_rs, z1_send, z1_recv, z1_ss, z1_rs)
    set2 = (y2_send, y2_recv, y2_ss, y2_rs, z2_send, z2_recv, z2_ss, z2_rs)

    loads[1].wait()
    loads[2].wait()
    att_mine = sum_over_col(
        lambda zz: dot(mix, wo[:, pl.ds(pl.multiple_of(zz * 256, 256), 256)]),
        hid[...].astype(F32), set1, "proj").astype(BF16)
    att[col] = att_mine

    def a_copy(slot, sem, dest):
        return rcopy(att.at[slot], att.at[slot], at_ss.at[sem], at_rs.at[slot], dest)

    a_sends = [(col, off, rem(z + off, nz) * 2 + ylo) for off in FAR_FIRST] + [(col, 0, ynb)]
    for a in a_sends:
        a_copy(*a).start()
    at_point("gather")
    for off in NEAR_FIRST:
        slot_z = rem(z + off, nz) * 2 + ylo
        a_copy(slot_z, 0, ynb).wait_recv()
        a_sends.append((slot_z, nz + off, ynb))
        a_copy(*a_sends[-1]).start()
    at_point("gather_y")
    for off in (0,) + NEAR_FIRST:
        a_copy(rem(z + off, nz) * 2 + 1 - ylo, 0, ynb).wait_recv()

    att_outs = [pltpu.make_async_copy(att.at[s], att_o.at[:, s * 128:(s + 1) * 128], out_sem.at[s])
                for s in range(ncol)]
    for c in att_outs:
        c.start()

    for c in own_loads:
        c.wait()
    sq = jnp.zeros((128, 128), F32)
    for s in range(ncol):
        a = att[s].astype(F32)
        sq = sq + a * a
    scale = lax.rsqrt(jnp.sum(sq, axis=1, keepdims=True) * (1.0 / (128 * ncol)) + 1e-06)
    at_point("gateup")
    ff = gv.shape[1]
    gate = jnp.zeros((128, ff), F32)
    up = jnp.zeros((128, ff), F32)
    for s in range(0, ncol, 2):
        a = jnp.concatenate([att[s], att[s + 1]], axis=1).astype(F32)
        n = (a * scale).astype(BF16)
        gate = gate + dot_nt(n, jnp.concatenate([gv[s], gv[s + 1]], axis=1))
        up = up + dot_nt(n, jnp.concatenate([uv[s], uv[s + 1]], axis=1))
    act[...] = (gate / (1.0 + jnp.exp(-gate)) * up).astype(BF16)

    at_point("down")
    blk[...] = sum_over_col(
        lambda zz: dot(act[...], jnp.concatenate([dv[zz * 2], dv[zz * 2 + 1]], axis=1)),
        att_mine.astype(F32), set2, "down").astype(BF16)
    blk_out = pltpu.make_async_copy(blk, blk_o, out_sem.at[ncol])
    blk_out.start()

    for t, owner, kind, dest, source in sent:
        wcopy(t, owner, kind, dest, source).wait_send()
    for i in range(steps):
        q_sends[i].wait_send()
        for hh in range(2):
            head = pair_at[i] * 2 + hh
            for c in o_copies(1, head):
                c.wait_send()

            @pl.when(head != col)
            def _():
                for c in o_copies(0, head):
                    c.wait_send()

    for bufs5 in (set1, set2):
        for off in range(nz):
            zz = rem(z + off, nz)
            y_copy(bufs5, zz).wait_send()
            if off:
                z_copy(bufs5, zz, z).wait_send()
    for a in a_sends:
        a_copy(*a).wait_send()
    for c in att_outs:
        c.wait()
    blk_out.wait()


def solution(mesh):
    ncol, nrow = mesh.shape["col"], mesh.shape["row"]
    nx = nrow // 4
    placed = (
        P("row", None), P("col", None, None), P("col"), P("col"), P(), P("row", None), P(),
        P("col", None), P("row", "col"), P("row", "col"), P("col", "row"),
    )

    def on_device(queries, pool, table, plen, off, hidden, lup, wo, gate, up, down):
        rows, d = hidden.shape
        gate, up = gate.T, up.T
        ff = gate.shape[0]
        nkeys = pool.shape[0] * pool.shape[1]
        dma, vm = pltpu.SemaphoreType.DMA, pltpu.VMEM
        anyspec = pl.BlockSpec(memory_space=pl.ANY)
        smem = pl.BlockSpec(memory_space=pltpu.SMEM)
        blocks, half = (ncol, rows, 128), (ncol // 2, rows, 128)
        steps = H // 4
        two = 2 * rows
        scratch = [
            vm(pool.shape, BF16), vm((steps, LATENT, 512), BF16), vm((steps, two, 2 * QK), BF16),
            vm((rows, 128), BF16), vm(wo.shape, BF16),
            vm((nrow,) + gate.shape, BF16), vm((nrow,) + up.shape, BF16), vm((nrow,) + down.shape, BF16),
            vm((2, nkeys, 256), BF16), vm((2, nkeys, 256), BF16),
            vm((2, nkeys, VDIM), BF16), vm((2, nkeys, VDIM), BF16),
            vm((two, nkeys), F32), vm((two, nkeys), F32), vm((1, nkeys), jnp.int32),
            vm((2,) + blocks, BF16), vm(blocks, BF16), vm((2, ncol, 8, 128), F32), vm((ncol, 8, 128), F32),
            vm(half, F32), vm(half, BF16), vm(half, BF16), vm(half, BF16), vm(half, BF16),
            vm(blocks, BF16), vm(half, BF16), vm(half, BF16), vm(half, BF16), vm(half, BF16),
            vm((rows, ff), BF16), vm((rows, 128), BF16),
            dma((3,)), dma((steps,)), dma((steps,)), dma((3,)), dma((ncol + 1,)), dma((3, 5, nrow)),
            dma((3, nrow)), dma((steps,)), dma((steps,)),
            dma((2, ncol)), dma((ncol,)), dma((2, ncol)), dma((ncol,)),
        ] + [dma((ncol // 2,))] * 4 + [dma((ncol,))] * 2 + [dma((ncol // 2,))] * 4
        return pl.pallas_call(
            functools.partial(kernel, ncol, nx),
            out_shape=(
                jax.ShapeDtypeStruct((rows, d), BF16),
                jax.ShapeDtypeStruct((rows, d // ncol), BF16),
            ),
            in_specs=[anyspec, anyspec, smem, smem, smem] + [anyspec] * 6,
            out_specs=(anyspec, anyspec),
            scratch_shapes=scratch,
            compiler_params=pltpu.CompilerParams(
                collective_id=0, has_side_effects=True, vmem_limit_bytes=60 << 20),
            name="block",
        )(queries, pool, table, plen, off, hidden, lup, wo, gate, up, down)

    return jax.shard_map(
        on_device, mesh=mesh, in_specs=placed,
        out_specs=(P("row", None), P("row", "col")), check_vma=False,
    )
```

```python
import functools
import math

import jax
import jax.numpy as jnp
from jax import lax
from jax.experimental import pallas as pl
from jax.experimental.pallas import tpu as pltpu
from jax.sharding import PartitionSpec as P

H = 16
NOPE = 128
ROPE = 64
VDIM = 128
LATENT = 512
QK = 192
MESH = pl.DeviceIdType.MESH
LOW = -1e30
FAR = 1 << 30
SCALE2 = math.log2(math.e) / math.sqrt(QK)
F32 = jnp.float32
BF16 = jnp.bfloat16
YP, XP, XM, SIB, DN = range(5)
KEY_CHUNK = 256
EXPAND = 512
LAG = 3
BEFORE = 3
FAR_FIRST = (4, 3, 5, 2, 6, 1, 7)
NEAR_FIRST = (1, 7, 2, 6, 3, 5, 4)


def dot(a, b):
    return jnp.dot(a, b, preferred_element_type=F32)


def dot_nt(a, b):
    return lax.dot_general(a, b, (((1,), (1,)), ((), ())), preferred_element_type=F32)


def kernel(
    ncol, nx,
    q_h, pool_h, table_s, plen_s, off_s, hid_h, lup_h, wo_h, g_h, u_h, d_h,
    att_o, blk_o,
    lat, lupv, q2, hid, wo, gv, uv, dv, keys_all, vals_all, sc0, sc1, pr0, pr1, kpos,
    o_send, o_recv, st_send, st_recv, own_term, y1_send, y1_recv, z1_send, z1_recv, att,
    y2_send, y2_recv, z2_send, z2_recv, act, blk,
    lsem, lup_sem, q_sem, own_sem, out_sem, ws_sem, wr_sem, wsib_sem, qs_sem, qr_sem,
    o_ss, o_rs, st_ss, st_rs, y1_ss, y1_rs, z1_ss, z1_rs, at_ss, at_rs, y2_ss, y2_rs, z2_ss, z2_rs,
):
    row, col = lax.axis_index("row"), lax.axis_index("col")

    def rem(a, b):
        return a % b

    def div(a, b):
        return a // b

    core, x, yhi = rem(row, 2), rem(div(row, 2), nx), div(row, 2 * nx)

    def row_of(yy, xx, cc):
        return (yy * nx + xx) * 2 + cc

    xp, xm, x2 = rem(x + 1, nx), rem(x + nx - 1, nx), rem(x + 2, nx)
    yo, co = 1 - yhi, 1 - core
    plus = [xp, xm, jnp.where(core == 0, xp, xm)]
    minus = [xm, xp, jnp.where(core == 0, xm, xp)]
    peers = [row_of(yo, x, core), row_of(yhi, xp, core), row_of(yhi, xm, core), row_of(yhi, x, co)]
    ups = [[row_of(yy, minus[t], core) for t in range(3)] for yy in (yhi, yo)]
    dns = [[row_of(yy, plus[t], core) for t in range(3)] for yy in (yhi, yo)]
    x2s = [row_of(yy, x2, core) for yy in (yhi, yo)]
    full = [gv, uv, dv]
    mine_h = [g_h, u_h, d_h]

    nz = ncol // 2
    z, ylo = div(col, 2), rem(col, 2)
    ynb = z * 2 + 1 - ylo
    sib = peers[SIB]
    steps = nz // 2
    turn = rem(core + z, 2)
    pair_at = [rem(z + 2 + 2 * i + turn, nz) for i in range(steps)]
    other_at = [rem(z + 2 + 2 * i + 1 - turn, nz) for i in range(steps)]

    loads = [
        pltpu.make_async_copy(pool_h, lat, lsem.at[0]),
        pltpu.make_async_copy(wo_h, wo, lsem.at[1]),
        pltpu.make_async_copy(hid_h.at[:, pl.ds(pl.multiple_of(col * 128, 128), 128)], hid, lsem.at[2]),
    ]

    def q_cols(p):
        return q_h.at[:, pl.ds(pl.multiple_of(p * 2 * QK, 2 * QK), 2 * QK)]

    lup_loads = [
        pltpu.make_async_copy(
            lup_h.at[:, pl.ds(pl.multiple_of(pair_at[i] * 512, 512), 512)], lupv.at[i], lup_sem.at[i])
        for i in range(steps)
    ]
    q_loads = [
        pltpu.make_async_copy(q_cols(pair_at[i]), q2.at[i, pl.ds(0, 128), :], q_sem.at[i])
        for i in range(steps)
    ]
    q_sends = [
        pltpu.make_async_remote_copy(
            src_ref=q_cols(other_at[i]), dst_ref=q2.at[i, pl.ds(128, 128), :],
            send_sem=qs_sem, recv_sem=qr_sem.at[i], device_id=(sib, col), device_id_type=MESH)
        for i in range(steps)
    ]
    lup_loads[0].start()
    loads[0].start()

    barrier = pltpu.get_barrier_semaphore()

    @pl.loop(1, ncol)
    def _(t):
        pl.semaphore_signal(barrier, inc=1, device_id=(row, rem(col + t, ncol)), device_id_type=MESH)

    @pl.loop(0, ncol)
    def _(t):
        pl.semaphore_signal(barrier, inc=1, device_id=(sib, rem(col + t, ncol)), device_id_type=MESH)

    for peer in peers[:SIB]:
        pl.semaphore_signal(barrier, inc=1, device_id=(peer, col), device_id_type=MESH)

    for c in q_loads + lup_loads[1:]:
        c.start()
    own_loads = [pltpu.make_async_copy(mine_h[t], full[t].at[row], own_sem.at[t]) for t in range(3)]
    for c in loads[1:] + own_loads:
        c.start()

    base = col * kpos.shape[1]
    lane = lax.broadcasted_iota(jnp.int32, kpos.shape, 1)
    page, slot = lax.shift_right_logical(lane, 6), lane & 63
    kp = jnp.full(kpos.shape, FAR, jnp.int32)
    for p in range(lat.shape[0]):
        here = jnp.where(slot < plen_s[p], base + p * 64 + slot, FAR)
        kp = jnp.where(page == table_s[p], here, kp)
    kpos[...] = kp
    sub = lax.broadcasted_iota(jnp.int32, (256, 1), 0)
    qpos = off_s[0] + jnp.where(sub < 128, row * 128 + sub, sib * 128 + sub - 128)

    nkeys = keys_all.shape[2]
    bufs = [(keys_all.at[i], vals_all.at[i]) for i in range(steps)]

    def expand(i, kc, size):
        keys, vals = bufs[i]
        rows = slice(kc * size, (kc + 1) * size)
        pages = slice(kc * size // 64, (kc + 1) * size // 64)
        e = dot(lat[pages, :, :LATENT].reshape(size, LATENT), lupv[i]).astype(BF16)
        keys[0, rows, :NOPE] = e[:, :128]
        vals[0, rows, :] = e[:, 128:256]
        keys[1, rows, :NOPE] = e[:, 256:384]
        vals[1, rows, :] = e[:, 384:]

    loads[0].wait()
    zeros64 = jnp.zeros((nkeys, 64), BF16)
    rope = jnp.concatenate([lat[:, :, LATENT:].reshape(nkeys, ROPE), zeros64], axis=1)
    for keys, _v in bufs:
        for hh in range(2):
            keys[hh, :, NOPE:] = rope

    def expand_pairs(first, last):
        for i in range(first, last):
            lup_loads[i].wait()
            for kc in range(nkeys // EXPAND):
                expand(i, kc, EXPAND)

    expand_pairs(0, BEFORE)

    pl.semaphore_wait(barrier, 2 * ncol - 1 + len(peers) - 1)
    for c in q_sends:
        c.start()

    def wcopy(t, owner, kind, dest, source=None):
        return pltpu.make_async_remote_copy(
            src_ref=full[t].at[owner] if source is None else source,
            dst_ref=full[t].at[owner],
            send_sem=ws_sem.at[t],
            recv_sem=wsib_sem.at[t] if kind == SIB else wr_sem.at[t, owner],
            device_id=(dest, col),
            device_id_type=MESH,
        )

    def wgroup(t, count):
        group = full[t].at[pl.ds(0, count)]
        return pltpu.make_async_remote_copy(
            src_ref=group, dst_ref=group, send_sem=ws_sem.at[t], recv_sem=wsib_sem.at[t],
            device_id=(sib, col), device_id_type=MESH)

    def wsend(t, owner, kind, dest, source=None):
        wcopy(t, owner, kind, dest, source).start()

    def warrive(t, owner):
        wcopy(t, owner, DN, sib).wait_recv()

    def stage_own(t):
        for kind in range(4):
            wsend(t, row, kind, peers[kind], mine_h[t])

    def stage_y(t):
        o = peers[YP]
        warrive(t, o)
        for kind in (XP, XM, SIB):
            wsend(t, o, kind, peers[kind])

    def stage_x(t, yy):
        up, dn = ups[yy][t], dns[yy][t]
        warrive(t, up)
        wsend(t, up, DN, dns[0][t])
        wsend(t, up, SIB, sib)
        warrive(t, dn)
        wsend(t, dn, SIB, sib)

    def stage_x2(t, yy):
        o = x2s[yy]
        warrive(t, o)
        wsend(t, o, SIB, sib)

    def stage_sib(t):
        wgroup(t, 2 * nx).wait_recv()

    plan = {
        "start": [(stage_own, 0), (stage_own, 1)],
        1: [(stage_x, 0, 0), (stage_x, 1, 0), (stage_own, 2)],
        3: [(stage_y, 0), (stage_y, 1)],
        "proj_z": [(stage_x, 2, 0), (stage_y, 2), (stage_x, 0, 1), (stage_x, 1, 1)],
        "gather": [(stage_x2, 0, 0), (stage_x2, 1, 0), (stage_x2, 0, 1), (stage_x2, 1, 1),
                   (stage_x, 2, 1), (stage_sib, 0), (stage_sib, 1)],
        "down": [(stage_x2, 2, 0), (stage_x2, 2, 1), (stage_sib, 2)],
    }

    def at_point(name):
        for stage, *which in plan.get(name, ()):
            stage(*which)

    at_point("start")
    expand_pairs(BEFORE, steps)

    def o_copies(part, head):
        dest = sib if part else row
        return (
            pltpu.make_async_remote_copy(
                src_ref=o_send.at[part, head], dst_ref=o_recv.at[col], send_sem=o_ss.at[part],
                recv_sem=o_rs, device_id=(dest, head), device_id_type=MESH),
            pltpu.make_async_remote_copy(
                src_ref=st_send.at[part, head], dst_ref=st_recv.at[col], send_sem=st_ss.at[part],
                recv_sem=st_rs, device_id=(dest, head), device_id_type=MESH),
        )

    lane128 = lax.broadcasted_iota(jnp.int32, (128, 128), 1)
    scs, prs = [sc0, sc1], [pr0, pr1]
    nchunk = nkeys // KEY_CHUNK
    mine = rem(div(col, 2) + core, 2) == 0
    for i in range(steps):
        keys, vals = bufs[i]
        q_loads[i].wait()
        q_sends[i].wait_recv()
        zq = jnp.zeros((256, 64), BF16)
        qs = [jnp.concatenate([q2[i, :, hh * QK:(hh + 1) * QK], zq], axis=1) for hh in range(2)]
        best = [jnp.full((256, 128), LOW, F32)] * 2
        for kc in range(nchunk):
            ks = slice(kc * KEY_CHUNK, (kc + 1) * KEY_CHUNK)
            for hh in range(2):
                s = dot_nt(qs[hh], keys[hh, ks, :])
                s = jnp.where(kpos[:, ks] <= qpos, s, LOW)
                scs[hh][:, ks] = s
                for j in range(KEY_CHUNK // 128):
                    best[hh] = jnp.maximum(best[hh], s[:, j * 128:(j + 1) * 128])
        ms = [jnp.max(b, axis=1, keepdims=True) for b in best]
        mc = [jnp.where(m < 0.1 * LOW, 0.0, m) * SCALE2 for m in ms]
        tot, out = [jnp.zeros((256, 128), F32)] * 2, [None, None]
        for hh in range(2):
            for kc in range(nchunk):
                ks = slice(kc * KEY_CHUNK, (kc + 1) * KEY_CHUNK)
                pr = jnp.exp2(scs[hh][:, ks] * SCALE2 - mc[hh])
                for j in range(KEY_CHUNK // 128):
                    tot[hh] = tot[hh] + pr[:, j * 128:(j + 1) * 128]
                prs[hh][:, ks] = pr.astype(BF16)
            out[hh] = dot(prs[hh][...], vals[hh])
        for hh in range(2):
            head = pair_at[i] * 2 + hh
            total = jnp.sum(tot[hh], axis=1, keepdims=True)
            for part in range(2):
                rs = slice(part * 128, (part + 1) * 128)
                stats = jnp.where(lane128 == 0, ms[hh][rs] * SCALE2, jnp.where(lane128 == 1, total[rs], 0.0))
                o_send[part, head] = out[hh][rs].astype(BF16)
                st_send[part, head] = stats.T[:8, :]
        for hh in range(2):
            head = pair_at[i] * 2 + hh
            for c in o_copies(1, head):
                c.start()

            @pl.when(head != col)
            def _():
                for c in o_copies(0, head):
                    c.start()

            @pl.when(head == col)
            def _():
                o_recv[col] = o_send[0, col]
                st_recv[col] = st_send[0, col]

        at_point(i)

    def o_group(part, count):
        o, st = o_recv.at[pl.ds(0, count)], st_recv.at[pl.ds(0, count)]
        return (
            pltpu.make_async_remote_copy(
                src_ref=o, dst_ref=o, send_sem=o_ss.at[part], recv_sem=o_rs,
                device_id=(sib, col), device_id_type=MESH),
            pltpu.make_async_remote_copy(
                src_ref=st, dst_ref=st, send_sem=st_ss.at[part], recv_sem=st_rs,
                device_id=(sib, col), device_id_type=MESH),
        )

    @pl.when(mine)
    def _():
        for c in o_group(0, ncol - 1):
            c.wait_recv()

    @pl.when(jnp.logical_not(mine))
    def _():
        for c in o_group(0, ncol):
            c.wait_recv()

    ms, ls = st_recv[:, 0, :], st_recv[:, 1, :]
    top = jnp.max(ms, axis=0, keepdims=True)
    wgt = jnp.exp2(ms - top)
    share = wgt / jnp.sum(wgt * ls, axis=0, keepdims=True)
    share = jnp.concatenate([share, jnp.zeros((128 - ncol, 128), F32)], axis=0).T
    mix = jnp.zeros((128, 128), F32)
    for s in range(ncol):
        mix = mix + share[:, s:s + 1] * o_recv[s].astype(F32)
    mix = mix.astype(BF16)

    def rcopy(src, dst, ss, rs, dest):
        return pltpu.make_async_remote_copy(
            src_ref=src, dst_ref=dst, send_sem=ss, recv_sem=rs, device_id=(row, dest), device_id_type=MESH)

    def y_copy(bufs5, zz):
        ys, yr, yss, yrs = bufs5[:4]
        return rcopy(ys.at[zz], yr.at[zz], yss, yrs.at[zz], ynb)

    def z_copy(bufs5, zz, mine_slot):
        zs, zr, zss, zrs = bufs5[4:]
        return rcopy(zs.at[zz], zr.at[mine_slot], zss, zrs.at[mine_slot], zz * 2 + ylo)

    def sum_over_col(term_of, start, bufs5, name):
        for off in FAR_FIRST + (0,):
            zz = rem(z + off, nz)
            both = term_of(zz)
            a, b = both[:, :128], both[:, 128:]
            own_term[zz] = jnp.where(ylo == 0, a, b)
            bufs5[0][zz] = jnp.where(ylo == 0, b, a).astype(BF16)
            y_copy(bufs5, zz).start()
        at_point(name + "_y")
        acc = start
        for off in FAR_FIRST + (0,):
            zz = rem(z + off, nz)
            y_copy(bufs5, zz).wait_recv()
            pair = own_term[zz] + bufs5[1][zz].astype(F32)
            if off:
                bufs5[4][zz] = pair.astype(BF16)
                z_copy(bufs5, zz, z).start()
            else:
                acc = acc + pair
        at_point(name + "_z")
        for off in NEAR_FIRST:
            zz = rem(z + off, nz)
            z_copy(bufs5, zz, zz).wait_recv()
            acc = acc + bufs5[5][zz].astype(F32)
        return acc

    set1 = (y1_send, y1_recv, y1_ss, y1_rs, z1_send, z1_recv, z1_ss, z1_rs)
    set2 = (y2_send, y2_recv, y2_ss, y2_rs, z2_send, z2_recv, z2_ss, z2_rs)

    loads[1].wait()
    loads[2].wait()
    att_mine = sum_over_col(
        lambda zz: dot(mix, wo[:, pl.ds(pl.multiple_of(zz * 256, 256), 256)]),
        hid[...].astype(F32), set1, "proj").astype(BF16)
    att[col] = att_mine

    def a_copy(slot, dest):
        return rcopy(att.at[slot], att.at[slot], at_ss, at_rs.at[slot], dest)

    for off in FAR_FIRST:
        a_copy(col, rem(z + off, nz) * 2 + ylo).start()
    a_copy(col, ynb).start()
    for c in own_loads:
        c.wait()
    at_point("gather")
    ff = gv.shape[1]
    gate = jnp.zeros((128, ff), F32)
    up = jnp.zeros((128, ff), F32)
    sq = jnp.zeros((128, 128), F32)
    order = (0,) + NEAR_FIRST
    for k in range(nz + LAG):
        if 0 < k < nz:
            slot = rem(z + order[k], nz) * 2 + ylo
            a_copy(slot, ynb).wait_recv()
            a_copy(slot, ynb).start()
        if k >= LAG:
            zz = rem(z + order[k - LAG], nz)
            a_copy(zz * 2 + 1 - ylo, ynb).wait_recv()
            pltpu.make_async_copy(
                att.at[zz * 2], att_o.at[:, pl.ds(pl.multiple_of(zz * 256, 256), 128)], out_sem.at[0]).start()
            pltpu.make_async_copy(
                att.at[zz * 2 + 1], att_o.at[:, pl.ds(pl.multiple_of(zz * 256 + 128, 128), 128)],
                out_sem.at[0]).start()
            n = jnp.concatenate([att[zz * 2], att[zz * 2 + 1]], axis=1)
            gate = gate + dot_nt(n, jnp.concatenate([gv[zz * 2], gv[zz * 2 + 1]], axis=1))
            up = up + dot_nt(n, jnp.concatenate([uv[zz * 2], uv[zz * 2 + 1]], axis=1))
            wide = n.astype(F32)
            wide = wide * wide
            sq = sq + wide[:, :128] + wide[:, 128:]
    scale = lax.rsqrt(jnp.sum(sq, axis=1, keepdims=True) * (1.0 / (128 * ncol)) + 1e-06)
    gate, up = gate * scale, up * scale
    act[...] = (gate / (1.0 + jnp.exp(-gate)) * up).astype(BF16)

    at_point("down")
    blk[...] = sum_over_col(
        lambda zz: dot(act[...], jnp.concatenate([dv[zz * 2], dv[zz * 2 + 1]], axis=1)),
        att_mine.astype(F32), set2, "down").astype(BF16)
    blk_out = pltpu.make_async_copy(blk, blk_o, out_sem.at[1])
    blk_out.start()

    for t in range(3):
        wgroup(t, 15).wait_send()
    q_all = q2.at[:, pl.ds(128, 128), :]
    pltpu.make_async_remote_copy(
        src_ref=q_all, dst_ref=q_all, send_sem=qs_sem, recv_sem=qr_sem.at[0],
        device_id=(sib, col), device_id_type=MESH).wait_send()
    for c in o_group(1, 2 * steps):
        c.wait_send()

    @pl.when(mine)
    def _():
        for c in o_group(0, 2 * steps - 1):
            c.wait_send()

    @pl.when(jnp.logical_not(mine))
    def _():
        for c in o_group(0, 2 * steps):
            c.wait_send()

    for ys, _yr, yss, yrs, zs, _zr, zss, zrs in (set1, set2):
        rcopy(ys, ys, yss, yrs.at[0], ynb).wait_send()
        most = zs.at[pl.ds(0, nz - 1)]
        rcopy(most, most, zss, zrs.at[0], ynb).wait_send()
    most = att.at[pl.ds(0, ncol - 1)]
    rcopy(most, most, at_ss, at_rs.at[0], ynb).wait_send()
    pltpu.make_async_copy(att_o, att_o, out_sem.at[0]).wait()
    blk_out.wait()


def write_out(a_h, b_h, a_o, b_o, a_v, b_v, sem):
    parts = 4
    size = a_v.shape[0] // parts

    def rows(ref, i):
        return ref.at[pl.ds(i * size, size), :]

    pieces = [(rows(a_h, i), rows(a_v, i), rows(a_o, i)) for i in range(parts)] + [(b_h, b_v, b_o)]
    ins = [pltpu.make_async_copy(h, v, sem.at[0, i]) for i, (h, v, o) in enumerate(pieces)]
    outs = [pltpu.make_async_copy(v, o, sem.at[1, i]) for i, (h, v, o) in enumerate(pieces)]
    for c in ins:
        c.start()
    for c, o in zip(ins, outs):
        c.wait()
        o.start()
    for o in outs:
        o.wait()


def solution(mesh):
    ncol, nrow = mesh.shape["col"], mesh.shape["row"]
    nx = nrow // 4
    placed = (
        P("row", None), P("col", None, None), P("col"), P("col"), P(), P("row", None), P(),
        P("col", None), P("row", "col"), P("row", "col"), P("col", "row"),
    )

    def on_device(queries, pool, table, plen, off, hidden, lup, wo, gate, up, down):
        rows, d = hidden.shape
        gate, up = gate.T, up.T
        ff = gate.shape[0]
        nkeys = pool.shape[0] * pool.shape[1]
        dma, vm = pltpu.SemaphoreType.DMA, pltpu.VMEM
        anyspec = pl.BlockSpec(memory_space=pl.ANY)
        smem = pl.BlockSpec(memory_space=pltpu.SMEM)
        blocks, half = (ncol, rows, 128), (ncol // 2, rows, 128)
        steps = H // 4
        two = 2 * rows
        scratch = [
            vm(pool.shape, BF16), vm((steps, LATENT, 512), BF16), vm((steps, two, 2 * QK), BF16),
            vm((rows, 128), BF16), vm(wo.shape, BF16),
            vm((nrow,) + gate.shape, BF16), vm((nrow,) + up.shape, BF16), vm((nrow,) + down.shape, BF16),
            vm((steps, 2, nkeys, 256), BF16), vm((steps, 2, nkeys, VDIM), BF16),
            vm((two, nkeys), F32), vm((two, nkeys), F32), vm((two, nkeys), BF16), vm((two, nkeys), BF16),
            vm((1, nkeys), jnp.int32),
            vm((2,) + blocks, BF16), vm(blocks, BF16), vm((2, ncol, 8, 128), F32), vm((ncol, 8, 128), F32),
            vm(half, F32), vm(half, BF16), vm(half, BF16), vm(half, BF16), vm(half, BF16),
            vm(blocks, BF16), vm(half, BF16), vm(half, BF16), vm(half, BF16), vm(half, BF16),
            vm((rows, ff), BF16), vm((rows, 128), BF16),
            dma((3,)), dma((steps,)), dma((steps,)), dma((3,)), dma((2,)), dma((3,)), dma((3, nrow)), dma((3,)),
            dma, dma((steps,)), dma((2,)), dma, dma((2,)), dma,
            dma, dma((ncol // 2,)), dma, dma((ncol // 2,)), dma, dma((ncol,)),
            dma, dma((ncol // 2,)), dma, dma((ncol // 2,)),
        ]
        att, blk = pl.pallas_call(
            functools.partial(kernel, ncol, nx),
            out_shape=(
                jax.ShapeDtypeStruct((rows, d), BF16),
                jax.ShapeDtypeStruct((rows, d // ncol), BF16),
            ),
            in_specs=[anyspec, anyspec, smem, smem, smem] + [anyspec] * 6,
            out_specs=(anyspec, anyspec),
            scratch_shapes=scratch,
            compiler_params=pltpu.CompilerParams(
                collective_id=0, has_side_effects=True, vmem_limit_bytes=60 << 20),
            name="block",
        )(queries, pool, table, plen, off, hidden, lup, wo, gate, up, down)
        return pl.pallas_call(
            write_out,
            out_shape=(
                jax.ShapeDtypeStruct(att.shape, BF16),
                jax.ShapeDtypeStruct(blk.shape, BF16),
            ),
            in_specs=[anyspec] * 2,
            out_specs=(anyspec, anyspec),
            scratch_shapes=[vm(att.shape, BF16), vm(blk.shape, BF16), dma((2, 5))],
            name="write_out",
        )(att, blk)

    return jax.shard_map(
        on_device, mesh=mesh, in_specs=placed,
        out_specs=(P("row", None), P("row", "col")), check_vma=False,
    )
```

```python
import functools
import math

import jax
import jax.numpy as jnp
from jax import lax
from jax.experimental import pallas as pl
from jax.experimental.pallas import tpu as pltpu
from jax.sharding import PartitionSpec as P

H = 16
NOPE = 128
ROPE = 64
VDIM = 128
LATENT = 512
QK = 192
MESH = pl.DeviceIdType.MESH
LOW = -1e30
FAR = 1 << 30
SCALE2 = math.log2(math.e) / math.sqrt(QK)
F32 = jnp.float32
BF16 = jnp.bfloat16
YP, XP, XM, SIB, DN = range(5)
KEY_CHUNK = 256
EXPAND = 512
LAG = 3
ROWS = 16
FAR_FIRST = (4, 3, 5, 2, 6, 1, 7)
NEAR_FIRST = (1, 7, 2, 6, 3, 5, 4)


def dot(a, b):
    return jnp.dot(a, b, preferred_element_type=F32)


def dot_nt(a, b):
    return lax.dot_general(a, b, (((1,), (1,)), ((), ())), preferred_element_type=F32)


def kernel(
    ncol, nx,
    q_h, pool_h, table_s, plen_s, off_s, hid_h, lup_h, wo_h, g_h, u_h, d_h,
    att_o, blk_o,
    lat, lupv, q2, hid, wo, gv, uv, dv, keys_all, vals_all, sc0, sc1, pr0, pr1, kpos, bias, bst, mx,
    o_send, o_recv, st_send, st_recv, own_term, y1_send, y1_recv, z1_send, z1_recv, att,
    y2_send, y2_recv, z2_send, z2_recv, act, blk,
    lsem, lup_sem, q_sem, own_sem, out_sem, ws_sem, wr_sem, wsib_sem, qs_sem, qr_sem,
    o_ss, o_rs, st_ss, st_rs, y1_ss, y1_rs, z1_ss, z1_rs, at_ss, at_rs, y2_ss, y2_rs, z2_ss, z2_rs,
):
    row, col = lax.axis_index("row"), lax.axis_index("col")

    def rem(a, b):
        return a % b

    def div(a, b):
        return a // b

    core, x, yhi = rem(row, 2), rem(div(row, 2), nx), div(row, 2 * nx)

    def row_of(yy, xx, cc):
        return (yy * nx + xx) * 2 + cc

    xp, xm, x2 = rem(x + 1, nx), rem(x + nx - 1, nx), rem(x + 2, nx)
    yo, co = 1 - yhi, 1 - core
    plus = [xp, xm, jnp.where(core == 0, xp, xm)]
    minus = [xm, xp, jnp.where(core == 0, xm, xp)]
    peers = [row_of(yo, x, core), row_of(yhi, xp, core), row_of(yhi, xm, core), row_of(yhi, x, co)]
    ups = [[row_of(yy, minus[t], core) for t in range(3)] for yy in (yhi, yo)]
    dns = [[row_of(yy, plus[t], core) for t in range(3)] for yy in (yhi, yo)]
    x2s = [row_of(yy, x2, core) for yy in (yhi, yo)]
    full = [gv, uv, dv]
    mine_h = [g_h, u_h, d_h]

    nz = ncol // 2
    z, ylo = div(col, 2), rem(col, 2)
    ynb = z * 2 + 1 - ylo
    sib = peers[SIB]
    steps = nz // 2
    turn = rem(core + z, 2)
    pair_at = [rem(z + 2 + 2 * i + turn, nz) for i in range(steps)]
    other_at = [rem(z + 2 + 2 * i + 1 - turn, nz) for i in range(steps)]

    loads = [
        pltpu.make_async_copy(pool_h, lat, lsem.at[0]),
        pltpu.make_async_copy(wo_h, wo, lsem.at[1]),
        pltpu.make_async_copy(hid_h.at[:, pl.ds(pl.multiple_of(col * 128, 128), 128)], hid, lsem.at[2]),
    ]

    def q_cols(p):
        return q_h.at[:, pl.ds(pl.multiple_of(p * 2 * QK, 2 * QK), 2 * QK)]

    lup_loads = [
        pltpu.make_async_copy(
            lup_h.at[:, pl.ds(pl.multiple_of(pair_at[i] * 512, 512), 512)], lupv.at[i], lup_sem.at[i])
        for i in range(steps)
    ]
    q_loads = [
        pltpu.make_async_copy(q_cols(pair_at[i]), q2.at[i, pl.ds(0, 128), :], q_sem.at[i])
        for i in range(steps)
    ]
    q_sends = [
        pltpu.make_async_remote_copy(
            src_ref=q_cols(other_at[i]), dst_ref=q2.at[i, pl.ds(128, 128), :],
            send_sem=qs_sem, recv_sem=qr_sem.at[i], device_id=(sib, col), device_id_type=MESH)
        for i in range(steps)
    ]
    lup_loads[0].start()
    loads[0].start()

    barrier = pltpu.get_barrier_semaphore()

    @pl.loop(1, ncol)
    def _(t):
        pl.semaphore_signal(barrier, inc=1, device_id=(row, rem(col + t, ncol)), device_id_type=MESH)

    @pl.loop(0, ncol)
    def _(t):
        pl.semaphore_signal(barrier, inc=1, device_id=(sib, rem(col + t, ncol)), device_id_type=MESH)

    for peer in peers[:SIB]:
        pl.semaphore_signal(barrier, inc=1, device_id=(peer, col), device_id_type=MESH)

    for c in q_loads + lup_loads[1:]:
        c.start()
    own_loads = [pltpu.make_async_copy(mine_h[t], full[t].at[row], own_sem.at[t]) for t in range(3)]
    for c in loads[1:] + own_loads:
        c.start()

    base = col * kpos.shape[1]
    lane = lax.broadcasted_iota(jnp.int32, kpos.shape, 1)
    page, slot = lax.shift_right_logical(lane, 6), lane & 63
    kp = jnp.full(kpos.shape, FAR, jnp.int32)
    for p in range(lat.shape[0]):
        here = jnp.where(slot < plen_s[p], base + p * 64 + slot, FAR)
        kp = jnp.where(page == table_s[p], here, kp)
    kpos[...] = kp
    sub = lax.broadcasted_iota(jnp.int32, (256, 1), 0)
    qpos = off_s[0] + jnp.where(sub < 128, row * 128 + sub, sib * 128 + sub - 128)

    nkeys = keys_all.shape[2]

    def make_bias():
        for rb in range(0, 256, 16):
            seen = kpos[...] <= qpos[rb:rb + 16]
            bias[rb:rb + 16, :] = jnp.where(seen, 0.0, LOW)

    bufs = [(keys_all.at[i], vals_all.at[i]) for i in range(steps)]

    def expand(i, kc, size):
        keys, vals = bufs[i]
        rows = slice(kc * size, (kc + 1) * size)
        pages = slice(kc * size // 64, (kc + 1) * size // 64)
        e = dot(lat[pages, :, :LATENT].reshape(size, LATENT), lupv[i]).astype(BF16)
        keys[0, rows, :NOPE] = e[:, :128]
        vals[0, rows, :] = e[:, 128:256]
        keys[1, rows, :NOPE] = e[:, 256:384]
        vals[1, rows, :] = e[:, 384:]

    pl.semaphore_wait(barrier, 2 * ncol - 1 + len(peers) - 1)
    for c in q_sends:
        c.start()

    def wcopy(t, owner, kind, dest, source=None):
        return pltpu.make_async_remote_copy(
            src_ref=full[t].at[owner] if source is None else source,
            dst_ref=full[t].at[owner],
            send_sem=ws_sem.at[t],
            recv_sem=wsib_sem.at[t] if kind == SIB else wr_sem.at[t, owner],
            device_id=(dest, col),
            device_id_type=MESH,
        )

    def wgroup(t, count):
        group = full[t].at[pl.ds(0, count)]
        return pltpu.make_async_remote_copy(
            src_ref=group, dst_ref=group, send_sem=ws_sem.at[t], recv_sem=wsib_sem.at[t],
            device_id=(sib, col), device_id_type=MESH)

    def wsend(t, owner, kind, dest, source=None):
        wcopy(t, owner, kind, dest, source).start()

    def warrive(t, owner):
        wcopy(t, owner, DN, sib).wait_recv()

    def stage_own(t):
        for kind in range(4):
            wsend(t, row, kind, peers[kind], mine_h[t])

    def stage_y(t):
        o = peers[YP]
        warrive(t, o)
        for kind in (XP, XM, SIB):
            wsend(t, o, kind, peers[kind])

    def stage_x(t, yy):
        up, dn = ups[yy][t], dns[yy][t]
        warrive(t, up)
        wsend(t, up, DN, dns[0][t])
        wsend(t, up, SIB, sib)
        warrive(t, dn)
        wsend(t, dn, SIB, sib)

    def stage_x2(t, yy):
        o = x2s[yy]
        warrive(t, o)
        wsend(t, o, SIB, sib)

    def stage_sib(t):
        wgroup(t, 2 * nx).wait_recv()

    plan = {
        "start": [(stage_own, 0), (stage_own, 1)],
        0: [(stage_x, 0, 0), (stage_x, 1, 0), (stage_own, 2)],
        2: [(stage_y, 0), (stage_y, 1)],
        3: [(stage_x, 2, 0)],
        "proj_y": [(stage_y, 2), (stage_x, 0, 1), (stage_x, 1, 1)],
        "proj_z": [(stage_x2, 0, 0), (stage_x2, 1, 0)],
        "gather": [(stage_x2, 0, 1), (stage_x2, 1, 1), (stage_x, 2, 1), (stage_sib, 0), (stage_sib, 1)],
        "down": [(stage_x2, 2, 0), (stage_x2, 2, 1), (stage_sib, 2)],
    }

    def at_point(name):
        for stage, *which in plan.get(name, ()):
            stage(*which)

    at_point("start")

    loads[0].wait()
    zeros64 = jnp.zeros((nkeys, 64), BF16)
    rope = jnp.concatenate([lat[:, :, LATENT:].reshape(nkeys, ROPE), zeros64], axis=1)
    for keys, _v in bufs:
        for hh in range(2):
            keys[hh, :, NOPE:] = rope


    def expand_pairs(first, last):
        for i in range(first, last):
            lup_loads[i].wait()
            for kc in range(nkeys // EXPAND):
                expand(i, kc, EXPAND)

    expand_pairs(0, steps)

    def o_copies(part, head):
        dest = sib if part else row
        return (
            pltpu.make_async_remote_copy(
                src_ref=o_send.at[part, head], dst_ref=o_recv.at[col], send_sem=o_ss.at[part],
                recv_sem=o_rs, device_id=(dest, head), device_id_type=MESH),
            pltpu.make_async_remote_copy(
                src_ref=st_send.at[part, head], dst_ref=st_recv.at[col], send_sem=st_ss.at[part],
                recv_sem=st_rs, device_id=(dest, head), device_id_type=MESH),
        )

    lane128 = lax.broadcasted_iota(jnp.int32, (128, 128), 1)
    scs, prs = [sc0, sc1], [pr0, pr1]
    nchunk = nkeys // KEY_CHUNK
    mine = rem(div(col, 2) + core, 2) == 0
    make_bias()
    for i in range(steps):
        q_loads[i].wait()
        q_sends[i].wait_recv()
    zq = jnp.zeros((256, 64), BF16)
    ones = jnp.ones((nkeys, 128), BF16)

    def score(n, kc):
        i, hh = n // 2, n % 2
        q = jnp.concatenate([q2[i, :, hh * QK:(hh + 1) * QK], zq], axis=1)
        ks = slice(kc * KEY_CHUNK, (kc + 1) * KEY_CHUNK)
        t = dot_nt(q, bufs[i][0][hh, ks, :]) * SCALE2 + bias[:, ks]
        scs[hh][:, ks] = t
        best = t[:, :128]
        for c in range(1, KEY_CHUNK // 128):
            best = jnp.maximum(best, t[:, c * 128:(c + 1) * 128])
        bst[hh] = best if kc == 0 else jnp.maximum(best, bst[hh])

    def soft(hh, rb):
        rows = slice(rb * ROWS, (rb + 1) * ROWS)
        m = mx[hh, rows, :]
        for c in range(nkeys // 128):
            ks = slice(c * 128, (c + 1) * 128)
            prs[hh][rows, ks] = jnp.exp2(scs[hh][rows, ks] - m).astype(BF16)

    for kc in range(nchunk):
        score(0, kc)
    for i in range(steps):
        for hh in range(2):
            n = 2 * i + hh
            m = jnp.max(bst[hh], axis=1, keepdims=True)
            mx[hh] = jnp.broadcast_to(jnp.where(m < 0.01 * LOW, 0.0, m), mx.shape[1:])
            for kc in range(nchunk):
                for rb in range(256 // ROWS // nchunk):
                    soft(hh, kc * (256 // ROWS // nchunk) + rb)
                if n + 1 < 2 * steps:
                    score(n + 1, kc)
            out = dot(prs[hh][...], jnp.concatenate([bufs[i][1][hh], ones], axis=1))
            head = pair_at[i] * 2 + hh
            for part in range(2):
                rs = slice(part * 128, (part + 1) * 128)
                total = out[rs, 128:]
                top = jnp.where(total > 0.0, mx[hh, rs, :], LOW)
                stats = jnp.where(lane128 == 0, top, jnp.where(lane128 == 1, total, 0.0))
                o_send[part, head] = out[rs, :128].astype(BF16)
                st_send[part, head] = stats.T[:8, :]
        for hh in range(2):
            head = pair_at[i] * 2 + hh
            for c in o_copies(1, head):
                c.start()

            @pl.when(head != col)
            def _():
                for c in o_copies(0, head):
                    c.start()

            @pl.when(head == col)
            def _():
                o_recv[col] = o_send[0, col]
                st_recv[col] = st_send[0, col]

        at_point(i)

    def o_group(part, count):
        o, st = o_recv.at[pl.ds(0, count)], st_recv.at[pl.ds(0, count)]
        return (
            pltpu.make_async_remote_copy(
                src_ref=o, dst_ref=o, send_sem=o_ss.at[part], recv_sem=o_rs,
                device_id=(sib, col), device_id_type=MESH),
            pltpu.make_async_remote_copy(
                src_ref=st, dst_ref=st, send_sem=st_ss.at[part], recv_sem=st_rs,
                device_id=(sib, col), device_id_type=MESH),
        )

    @pl.when(mine)
    def _():
        for c in o_group(0, ncol - 1):
            c.wait_recv()

    @pl.when(jnp.logical_not(mine))
    def _():
        for c in o_group(0, ncol):
            c.wait_recv()

    ms, ls = st_recv[:, 0, :], st_recv[:, 1, :]
    top = jnp.max(ms, axis=0, keepdims=True)
    wgt = jnp.exp2(ms - top)
    share = wgt / jnp.sum(wgt * ls, axis=0, keepdims=True)
    share = jnp.concatenate([share, jnp.zeros((128 - ncol, 128), F32)], axis=0).T
    mix = jnp.zeros((128, 128), F32)
    for s in range(ncol):
        mix = mix + share[:, s:s + 1] * o_recv[s].astype(F32)
    mix = mix.astype(BF16)

    def rcopy(src, dst, ss, rs, dest):
        return pltpu.make_async_remote_copy(
            src_ref=src, dst_ref=dst, send_sem=ss, recv_sem=rs, device_id=(row, dest), device_id_type=MESH)

    def y_copy(bufs5, zz):
        ys, yr, yss, yrs = bufs5[:4]
        return rcopy(ys.at[zz], yr.at[zz], yss, yrs.at[zz], ynb)

    def z_copy(bufs5, zz, mine_slot):
        zs, zr, zss, zrs = bufs5[4:]
        return rcopy(zs.at[zz], zr.at[mine_slot], zss, zrs.at[mine_slot], zz * 2 + ylo)

    def sum_over_col(term_of, start, bufs5, name):
        for off in FAR_FIRST + (0,):
            zz = rem(z + off, nz)
            both = term_of(zz)
            a, b = both[:, :128], both[:, 128:]
            own_term[zz] = jnp.where(ylo == 0, a, b)
            bufs5[0][zz] = jnp.where(ylo == 0, b, a).astype(BF16)
            y_copy(bufs5, zz).start()
        at_point(name + "_y")
        acc = start
        for off in FAR_FIRST + (0,):
            zz = rem(z + off, nz)
            y_copy(bufs5, zz).wait_recv()
            pair = own_term[zz] + bufs5[1][zz].astype(F32)
            if off:
                bufs5[4][zz] = pair.astype(BF16)
                z_copy(bufs5, zz, z).start()
            else:
                acc = acc + pair
        at_point(name + "_z")
        for off in NEAR_FIRST:
            zz = rem(z + off, nz)
            z_copy(bufs5, zz, zz).wait_recv()
            acc = acc + bufs5[5][zz].astype(F32)
        return acc

    set1 = (y1_send, y1_recv, y1_ss, y1_rs, z1_send, z1_recv, z1_ss, z1_rs)
    set2 = (y2_send, y2_recv, y2_ss, y2_rs, z2_send, z2_recv, z2_ss, z2_rs)

    loads[1].wait()
    loads[2].wait()
    att_mine = sum_over_col(
        lambda zz: dot(mix, wo[:, pl.ds(pl.multiple_of(zz * 256, 256), 256)]),
        hid[...].astype(F32), set1, "proj").astype(BF16)
    att[col] = att_mine

    def a_copy(slot, dest):
        return rcopy(att.at[slot], att.at[slot], at_ss, at_rs.at[slot], dest)

    for off in FAR_FIRST:
        a_copy(col, rem(z + off, nz) * 2 + ylo).start()
    a_copy(col, ynb).start()
    for c in own_loads:
        c.wait()
    at_point("gather")
    ff = gv.shape[1]
    gate = jnp.zeros((128, ff), F32)
    up = jnp.zeros((128, ff), F32)
    sq = jnp.zeros((128, 128), F32)
    order = (0,) + NEAR_FIRST
    for k in range(nz + LAG):
        if 0 < k < nz:
            slot = rem(z + order[k], nz) * 2 + ylo
            a_copy(slot, ynb).wait_recv()
            a_copy(slot, ynb).start()
        if k >= LAG:
            zz = rem(z + order[k - LAG], nz)
            a_copy(zz * 2 + 1 - ylo, ynb).wait_recv()
            pltpu.make_async_copy(
                att.at[zz * 2], att_o.at[:, pl.ds(pl.multiple_of(zz * 256, 256), 128)], out_sem.at[0]).start()
            pltpu.make_async_copy(
                att.at[zz * 2 + 1], att_o.at[:, pl.ds(pl.multiple_of(zz * 256 + 128, 128), 128)],
                out_sem.at[0]).start()
            n = jnp.concatenate([att[zz * 2], att[zz * 2 + 1]], axis=1)
            gate = gate + dot_nt(n, jnp.concatenate([gv[zz * 2], gv[zz * 2 + 1]], axis=1))
            up = up + dot_nt(n, jnp.concatenate([uv[zz * 2], uv[zz * 2 + 1]], axis=1))
            wide = n.astype(F32)
            wide = wide * wide
            sq = sq + wide[:, :128] + wide[:, 128:]
    scale = lax.rsqrt(jnp.sum(sq, axis=1, keepdims=True) * (1.0 / (128 * ncol)) + 1e-06)
    gate, up = gate * scale, up * scale
    act[...] = (gate / (1.0 + jnp.exp(-gate)) * up).astype(BF16)

    at_point("down")
    blk[...] = sum_over_col(
        lambda zz: dot(act[...], jnp.concatenate([dv[zz * 2], dv[zz * 2 + 1]], axis=1)),
        att_mine.astype(F32), set2, "down").astype(BF16)
    blk_out = pltpu.make_async_copy(blk, blk_o, out_sem.at[1])
    blk_out.start()

    for t in range(3):
        wgroup(t, 15).wait_send()
    q_all = q2.at[:, pl.ds(128, 128), :]
    pltpu.make_async_remote_copy(
        src_ref=q_all, dst_ref=q_all, send_sem=qs_sem, recv_sem=qr_sem.at[0],
        device_id=(sib, col), device_id_type=MESH).wait_send()
    for c in o_group(1, 2 * steps):
        c.wait_send()

    @pl.when(mine)
    def _():
        for c in o_group(0, 2 * steps - 1):
            c.wait_send()

    @pl.when(jnp.logical_not(mine))
    def _():
        for c in o_group(0, 2 * steps):
            c.wait_send()

    for ys, _yr, yss, yrs, zs, _zr, zss, zrs in (set1, set2):
        rcopy(ys, ys, yss, yrs.at[0], ynb).wait_send()
        most = zs.at[pl.ds(0, nz - 1)]
        rcopy(most, most, zss, zrs.at[0], ynb).wait_send()
    most = att.at[pl.ds(0, ncol - 1)]
    rcopy(most, most, at_ss, at_rs.at[0], ynb).wait_send()
    pltpu.make_async_copy(att_o, att_o, out_sem.at[0]).wait()
    blk_out.wait()


def write_out(a_h, b_h, a_o, b_o, a_v, b_v, sem):
    parts = 4
    size = a_v.shape[0] // parts

    def rows(ref, i):
        return ref.at[pl.ds(i * size, size), :]

    pieces = [(rows(a_h, i), rows(a_v, i), rows(a_o, i)) for i in range(parts)] + [(b_h, b_v, b_o)]
    ins = [pltpu.make_async_copy(h, v, sem.at[0, i]) for i, (h, v, o) in enumerate(pieces)]
    outs = [pltpu.make_async_copy(v, o, sem.at[1, i]) for i, (h, v, o) in enumerate(pieces)]
    for c in ins:
        c.start()
    for c, o in zip(ins, outs):
        c.wait()
        o.start()
    for o in outs:
        o.wait()


def solution(mesh):
    ncol, nrow = mesh.shape["col"], mesh.shape["row"]
    nx = nrow // 4
    placed = (
        P("row", None), P("col", None, None), P("col"), P("col"), P(), P("row", None), P(),
        P("col", None), P("row", "col"), P("row", "col"), P("col", "row"),
    )

    def on_device(queries, pool, table, plen, off, hidden, lup, wo, gate, up, down):
        rows, d = hidden.shape
        gate, up = gate.T, up.T
        ff = gate.shape[0]
        nkeys = pool.shape[0] * pool.shape[1]
        dma, vm = pltpu.SemaphoreType.DMA, pltpu.VMEM
        anyspec = pl.BlockSpec(memory_space=pl.ANY)
        smem = pl.BlockSpec(memory_space=pltpu.SMEM)
        blocks, half = (ncol, rows, 128), (ncol // 2, rows, 128)
        steps = H // 4
        two = 2 * rows
        scratch = [
            vm(pool.shape, BF16), vm((steps, LATENT, 512), BF16), vm((steps, two, 2 * QK), BF16),
            vm((rows, 128), BF16), vm(wo.shape, BF16),
            vm((nrow,) + gate.shape, BF16), vm((nrow,) + up.shape, BF16), vm((nrow,) + down.shape, BF16),
            vm((steps, 2, nkeys, 256), BF16), vm((steps, 2, nkeys, VDIM), BF16),
            vm((two, nkeys), F32), vm((two, nkeys), F32), vm((two, nkeys), BF16), vm((two, nkeys), BF16),
            vm((1, nkeys), jnp.int32), vm((two, nkeys), F32),
            vm((2, two, 128), F32), vm((2, two, 128), F32),
            vm((2,) + blocks, BF16), vm(blocks, BF16), vm((2, ncol, 8, 128), F32), vm((ncol, 8, 128), F32),
            vm(half, F32), vm(half, BF16), vm(half, BF16), vm(half, BF16), vm(half, BF16),
            vm(blocks, BF16), vm(half, BF16), vm(half, BF16), vm(half, BF16), vm(half, BF16),
            vm((rows, ff), BF16), vm((rows, 128), BF16),
            dma((3,)), dma((steps,)), dma((steps,)), dma((3,)), dma((2,)), dma((3,)), dma((3, nrow)), dma((3,)),
            dma, dma((steps,)), dma((2,)), dma, dma((2,)), dma,
            dma, dma((ncol // 2,)), dma, dma((ncol // 2,)), dma, dma((ncol,)),
            dma, dma((ncol // 2,)), dma, dma((ncol // 2,)),
        ]
        att, blk = pl.pallas_call(
            functools.partial(kernel, ncol, nx),
            out_shape=(
                jax.ShapeDtypeStruct((rows, d), BF16),
                jax.ShapeDtypeStruct((rows, d // ncol), BF16),
            ),
            in_specs=[anyspec, anyspec, smem, smem, smem] + [anyspec] * 6,
            out_specs=(anyspec, anyspec),
            scratch_shapes=scratch,
            compiler_params=pltpu.CompilerParams(
                collective_id=0, has_side_effects=True, vmem_limit_bytes=60 << 20),
            name="block",
        )(queries, pool, table, plen, off, hidden, lup, wo, gate, up, down)
        return pl.pallas_call(
            write_out,
            out_shape=(
                jax.ShapeDtypeStruct(att.shape, BF16),
                jax.ShapeDtypeStruct(blk.shape, BF16),
            ),
            in_specs=[anyspec] * 2,
            out_specs=(anyspec, anyspec),
            scratch_shapes=[vm(att.shape, BF16), vm(blk.shape, BF16), dma((2, 5))],
            name="write_out",
        )(att, blk)

    return jax.shard_map(
        on_device, mesh=mesh, in_specs=placed,
        out_specs=(P("row", None), P("row", "col")), check_vma=False,
    )
```

```python
import functools
import math

import jax
import jax.numpy as jnp
from jax import lax
from jax.experimental import pallas as pl
from jax.experimental.pallas import tpu as pltpu
from jax.sharding import PartitionSpec as P

H = 16
NOPE = 128
ROPE = 64
VDIM = 128
LATENT = 512
QK = 192
MESH = pl.DeviceIdType.MESH
LOW = -1e30
FAR = 1 << 30
SCALE2 = math.log2(math.e) / math.sqrt(QK)
F32 = jnp.float32
BF16 = jnp.bfloat16
YP, XP, XM, SIB, DN = range(5)
KEY_CHUNK = 256
EXPAND = 512
LAG = 3
ROWS = 16
BEFORE = 2
FAR_FIRST = (4, 3, 5, 2, 6, 1, 7)
NEAR_FIRST = (1, 7, 2, 6, 3, 5, 4)


def dot(a, b):
    return jnp.dot(a, b, preferred_element_type=F32)


def dot_nt(a, b):
    return lax.dot_general(a, b, (((1,), (1,)), ((), ())), preferred_element_type=F32)


def kernel(
    ncol, nx,
    q_h, pool_h, table_s, plen_s, off_s, hid_h, lup_h, wo_h, g_h, u_h, d_h,
    att_o, blk_o,
    lat, lupv, q2, hid, wo, gv, uv, dv, keys_all, vals_all, sc0, sc1, pr0, pr1, kpos, bias, bst, mx,
    o_send, o_recv, st_send, st_recv, own_term, y1_send, y1_recv, z1_send, z1_recv, att,
    y2_send, y2_recv, z2_send, z2_recv, act, blk,
    lsem, lup_sem, q_sem, own_sem, out_sem, ws_sem, wr_sem, wsib_sem, qs_sem, qr_sem,
    o_ss, o_rs, st_ss, st_rs, y1_ss, y1_rs, z1_ss, z1_rs, at_ss, at_rs, y2_ss, y2_rs, z2_ss, z2_rs,
):
    row, col = lax.axis_index("row"), lax.axis_index("col")

    def rem(a, b):
        return a % b

    def div(a, b):
        return a // b

    core, x, yhi = rem(row, 2), rem(div(row, 2), nx), div(row, 2 * nx)

    def row_of(yy, xx, cc):
        return (yy * nx + xx) * 2 + cc

    xp, xm, x2 = rem(x + 1, nx), rem(x + nx - 1, nx), rem(x + 2, nx)
    yo, co = 1 - yhi, 1 - core
    plus = [xp, xm, jnp.where(core == 0, xp, xm)]
    minus = [xm, xp, jnp.where(core == 0, xm, xp)]
    peers = [row_of(yo, x, core), row_of(yhi, xp, core), row_of(yhi, xm, core), row_of(yhi, x, co)]
    ups = [[row_of(yy, minus[t], core) for t in range(3)] for yy in (yhi, yo)]
    dns = [[row_of(yy, plus[t], core) for t in range(3)] for yy in (yhi, yo)]
    x2s = [row_of(yy, x2, core) for yy in (yhi, yo)]
    full = [gv, uv, dv]
    mine_h = [g_h, u_h, d_h]

    nz = ncol // 2
    z, ylo = div(col, 2), rem(col, 2)
    ynb = z * 2 + 1 - ylo
    sib = peers[SIB]
    steps = nz // 2
    turn = rem(core + z, 2)
    pair_at = [rem(z + 2 + 2 * i + turn, nz) for i in range(steps)]
    other_at = [rem(z + 2 + 2 * i + 1 - turn, nz) for i in range(steps)]

    loads = [
        pltpu.make_async_copy(pool_h, lat, lsem.at[0]),
        pltpu.make_async_copy(wo_h, wo, lsem.at[1]),
        pltpu.make_async_copy(hid_h.at[:, pl.ds(pl.multiple_of(col * 128, 128), 128)], hid, lsem.at[2]),
    ]

    def q_cols(p):
        return q_h.at[:, pl.ds(pl.multiple_of(p * 2 * QK, 2 * QK), 2 * QK)]

    lup_loads = [
        pltpu.make_async_copy(
            lup_h.at[:, pl.ds(pl.multiple_of(pair_at[i] * 512, 512), 512)], lupv.at[i], lup_sem.at[i])
        for i in range(steps)
    ]
    q_loads = [
        pltpu.make_async_copy(q_cols(pair_at[i]), q2.at[i, pl.ds(0, 128), :], q_sem.at[i])
        for i in range(steps)
    ]
    q_sends = [
        pltpu.make_async_remote_copy(
            src_ref=q_cols(other_at[i]), dst_ref=q2.at[i, pl.ds(128, 128), :],
            send_sem=qs_sem, recv_sem=qr_sem.at[i], device_id=(sib, col), device_id_type=MESH)
        for i in range(steps)
    ]
    lup_loads[0].start()
    loads[0].start()

    barrier = pltpu.get_barrier_semaphore()

    @pl.loop(1, ncol)
    def _(t):
        pl.semaphore_signal(barrier, inc=1, device_id=(row, rem(col + t, ncol)), device_id_type=MESH)

    @pl.loop(0, ncol)
    def _(t):
        pl.semaphore_signal(barrier, inc=1, device_id=(sib, rem(col + t, ncol)), device_id_type=MESH)

    for peer in peers[:SIB]:
        pl.semaphore_signal(barrier, inc=1, device_id=(peer, col), device_id_type=MESH)

    for c in q_loads + lup_loads[1:]:
        c.start()
    own_loads = [pltpu.make_async_copy(mine_h[t], full[t].at[row], own_sem.at[t]) for t in range(3)]
    for c in loads[1:] + own_loads:
        c.start()

    base = col * kpos.shape[1]
    lane = lax.broadcasted_iota(jnp.int32, kpos.shape, 1)
    page, slot = lax.shift_right_logical(lane, 6), lane & 63
    kp = jnp.full(kpos.shape, FAR, jnp.int32)
    for p in range(lat.shape[0]):
        here = jnp.where(slot < plen_s[p], base + p * 64 + slot, FAR)
        kp = jnp.where(page == table_s[p], here, kp)
    kpos[...] = kp
    sub = lax.broadcasted_iota(jnp.int32, (256, 1), 0)
    qpos = off_s[0] + jnp.where(sub < 128, row * 128 + sub, sib * 128 + sub - 128)

    nkeys = keys_all.shape[2]

    def make_bias():
        for rb in range(0, 256, 16):
            seen = kpos[...] <= qpos[rb:rb + 16]
            bias[rb:rb + 16, :] = jnp.where(seen, 0.0, LOW)

    bufs = [(keys_all.at[i], vals_all.at[i]) for i in range(steps)]

    def expand(i, kc, size):
        keys, vals = bufs[i]
        rows = slice(kc * size, (kc + 1) * size)
        pages = slice(kc * size // 64, (kc + 1) * size // 64)
        e = dot(lat[pages, :, :LATENT].reshape(size, LATENT), lupv[i]).astype(BF16)
        keys[0, rows, :NOPE] = e[:, :128]
        vals[0, rows, :] = e[:, 128:256]
        keys[1, rows, :NOPE] = e[:, 256:384]
        vals[1, rows, :] = e[:, 384:]

    make_bias()
    loads[0].wait()
    zeros64 = jnp.zeros((nkeys, 64), BF16)
    rope = jnp.concatenate([lat[:, :, LATENT:].reshape(nkeys, ROPE), zeros64], axis=1)
    for keys, _v in bufs:
        for hh in range(2):
            keys[hh, :, NOPE:] = rope


    def expand_pairs(first, last):
        for i in range(first, last):
            lup_loads[i].wait()
            for kc in range(nkeys // EXPAND):
                expand(i, kc, EXPAND)

    expand_pairs(0, BEFORE)

    pl.semaphore_wait(barrier, 2 * ncol - 1 + len(peers) - 1)
    for c in q_sends:
        c.start()

    def wcopy(t, owner, kind, dest, source=None):
        return pltpu.make_async_remote_copy(
            src_ref=full[t].at[owner] if source is None else source,
            dst_ref=full[t].at[owner],
            send_sem=ws_sem.at[t],
            recv_sem=wsib_sem.at[t] if kind == SIB else wr_sem.at[t, owner],
            device_id=(dest, col),
            device_id_type=MESH,
        )

    def wgroup(t, count):
        group = full[t].at[pl.ds(0, count)]
        return pltpu.make_async_remote_copy(
            src_ref=group, dst_ref=group, send_sem=ws_sem.at[t], recv_sem=wsib_sem.at[t],
            device_id=(sib, col), device_id_type=MESH)

    def wsend(t, owner, kind, dest, source=None):
        wcopy(t, owner, kind, dest, source).start()

    def warrive(t, owner):
        wcopy(t, owner, DN, sib).wait_recv()

    def stage_own(t):
        for kind in range(4):
            wsend(t, row, kind, peers[kind], mine_h[t])

    def stage_y(t):
        o = peers[YP]
        warrive(t, o)
        for kind in (XP, XM, SIB):
            wsend(t, o, kind, peers[kind])

    def stage_x(t, yy):
        up, dn = ups[yy][t], dns[yy][t]
        warrive(t, up)
        wsend(t, up, DN, dns[0][t])
        wsend(t, up, SIB, sib)
        warrive(t, dn)
        wsend(t, dn, SIB, sib)

    def stage_x2(t, yy):
        o = x2s[yy]
        warrive(t, o)
        wsend(t, o, SIB, sib)

    def stage_sib(t):
        wgroup(t, 2 * nx).wait_recv()

    plan = {
        "start": [(stage_own, 0), (stage_own, 1), (stage_own, 2)],
        1: [(stage_x, 0, 0), (stage_x, 1, 0)],
        3: [(stage_y, 0), (stage_y, 1), (stage_x, 2, 0)],
        "proj_z": [(stage_y, 2)],
        "gather": [(stage_x, 0, 1), (stage_x, 1, 1), (stage_x2, 0, 0), (stage_x2, 1, 0)],
        "block0": [(stage_x2, 0, 1), (stage_x2, 1, 1), (stage_sib, 0), (stage_sib, 1)],
        "block4": [(stage_x, 2, 1)],
        "down": [(stage_x2, 2, 0), (stage_x2, 2, 1), (stage_sib, 2)],
    }

    def at_point(name):
        for stage, *which in plan.get(name, ()):
            stage(*which)

    at_point("start")

    expand_pairs(BEFORE, steps)

    def o_copies(part, head):
        dest = sib if part else row
        return (
            pltpu.make_async_remote_copy(
                src_ref=o_send.at[part, head], dst_ref=o_recv.at[col], send_sem=o_ss.at[part],
                recv_sem=o_rs, device_id=(dest, head), device_id_type=MESH),
            pltpu.make_async_remote_copy(
                src_ref=st_send.at[part, head], dst_ref=st_recv.at[col], send_sem=st_ss.at[part],
                recv_sem=st_rs, device_id=(dest, head), device_id_type=MESH),
        )

    lane128 = lax.broadcasted_iota(jnp.int32, (128, 128), 1)
    scs, prs = [sc0, sc1], [pr0, pr1]
    nchunk = nkeys // KEY_CHUNK
    mine = rem(div(col, 2) + core, 2) == 0
    for i in range(steps):
        q_loads[i].wait()
        q_sends[i].wait_recv()
    zq = jnp.zeros((256, 64), BF16)
    ones = jnp.ones((nkeys, 128), BF16)

    def score(n, kc):
        i, hh = n // 2, n % 2
        q = jnp.concatenate([q2[i, :, hh * QK:(hh + 1) * QK], zq], axis=1)
        ks = slice(kc * KEY_CHUNK, (kc + 1) * KEY_CHUNK)
        t = dot_nt(q, bufs[i][0][hh, ks, :]) * SCALE2 + bias[:, ks]
        scs[hh][:, ks] = t
        best = t[:, :128]
        for c in range(1, KEY_CHUNK // 128):
            best = jnp.maximum(best, t[:, c * 128:(c + 1) * 128])
        bst[hh] = best if kc == 0 else jnp.maximum(best, bst[hh])

    def soft(hh, rb):
        rows = slice(rb * ROWS, (rb + 1) * ROWS)
        m = mx[hh, rows, :]
        for c in range(nkeys // 128):
            ks = slice(c * 128, (c + 1) * 128)
            prs[hh][rows, ks] = jnp.exp2(scs[hh][rows, ks] - m).astype(BF16)

    for kc in range(nchunk):
        score(0, kc)
    for i in range(steps):
        for hh in range(2):
            n = 2 * i + hh
            m = jnp.max(bst[hh], axis=1, keepdims=True)
            mx[hh] = jnp.broadcast_to(jnp.where(m < 0.01 * LOW, 0.0, m), mx.shape[1:])
            for kc in range(nchunk):
                for rb in range(256 // ROWS // nchunk):
                    soft(hh, kc * (256 // ROWS // nchunk) + rb)
                if n + 1 < 2 * steps:
                    score(n + 1, kc)
            out = dot(prs[hh][...], jnp.concatenate([bufs[i][1][hh], ones], axis=1))
            head = pair_at[i] * 2 + hh
            for part in range(2):
                rs = slice(part * 128, (part + 1) * 128)
                total = out[rs, 128:]
                top = jnp.where(total > 0.0, mx[hh, rs, :], LOW)
                stats = jnp.where(lane128 == 0, top, jnp.where(lane128 == 1, total, 0.0))
                o_send[part, head] = out[rs, :128].astype(BF16)
                st_send[part, head] = stats.T[:8, :]
        for hh in range(2):
            head = pair_at[i] * 2 + hh
            for c in o_copies(1, head):
                c.start()

            @pl.when(head != col)
            def _():
                for c in o_copies(0, head):
                    c.start()

            @pl.when(head == col)
            def _():
                o_recv[col] = o_send[0, col]
                st_recv[col] = st_send[0, col]

        at_point(i)

    def o_group(part, count):
        o, st = o_recv.at[pl.ds(0, count)], st_recv.at[pl.ds(0, count)]
        return (
            pltpu.make_async_remote_copy(
                src_ref=o, dst_ref=o, send_sem=o_ss.at[part], recv_sem=o_rs,
                device_id=(sib, col), device_id_type=MESH),
            pltpu.make_async_remote_copy(
                src_ref=st, dst_ref=st, send_sem=st_ss.at[part], recv_sem=st_rs,
                device_id=(sib, col), device_id_type=MESH),
        )

    @pl.when(mine)
    def _():
        for c in o_group(0, ncol - 1):
            c.wait_recv()

    @pl.when(jnp.logical_not(mine))
    def _():
        for c in o_group(0, ncol):
            c.wait_recv()

    ms, ls = st_recv[:, 0, :], st_recv[:, 1, :]
    top = jnp.max(ms, axis=0, keepdims=True)
    wgt = jnp.exp2(ms - top)
    share = wgt / jnp.sum(wgt * ls, axis=0, keepdims=True)
    share = jnp.concatenate([share, jnp.zeros((128 - ncol, 128), F32)], axis=0).T
    mix = jnp.zeros((128, 128), F32)
    for s in range(ncol):
        mix = mix + share[:, s:s + 1] * o_recv[s].astype(F32)
    mix = mix.astype(BF16)

    def rcopy(src, dst, ss, rs, dest):
        return pltpu.make_async_remote_copy(
            src_ref=src, dst_ref=dst, send_sem=ss, recv_sem=rs, device_id=(row, dest), device_id_type=MESH)

    def y_copy(bufs5, zz):
        ys, yr, yss, yrs = bufs5[:4]
        return rcopy(ys.at[zz], yr.at[zz], yss, yrs.at[zz], ynb)

    def z_copy(bufs5, zz, mine_slot):
        zs, zr, zss, zrs = bufs5[4:]
        return rcopy(zs.at[zz], zr.at[mine_slot], zss, zrs.at[mine_slot], zz * 2 + ylo)

    def sum_over_col(term_of, start, bufs5, name):
        for off in FAR_FIRST + (0,):
            zz = rem(z + off, nz)
            both = term_of(zz)
            a, b = both[:, :128], both[:, 128:]
            own_term[zz] = jnp.where(ylo == 0, a, b)
            bufs5[0][zz] = jnp.where(ylo == 0, b, a).astype(BF16)
            y_copy(bufs5, zz).start()
        at_point(name + "_y")
        acc = start
        for off in FAR_FIRST + (0,):
            zz = rem(z + off, nz)
            y_copy(bufs5, zz).wait_recv()
            pair = own_term[zz] + bufs5[1][zz].astype(F32)
            if off:
                bufs5[4][zz] = pair.astype(BF16)
                z_copy(bufs5, zz, z).start()
            else:
                acc = acc + pair
        at_point(name + "_z")
        for off in NEAR_FIRST:
            zz = rem(z + off, nz)
            z_copy(bufs5, zz, zz).wait_recv()
            acc = acc + bufs5[5][zz].astype(F32)
        return acc

    set1 = (y1_send, y1_recv, y1_ss, y1_rs, z1_send, z1_recv, z1_ss, z1_rs)
    set2 = (y2_send, y2_recv, y2_ss, y2_rs, z2_send, z2_recv, z2_ss, z2_rs)

    loads[1].wait()
    loads[2].wait()
    att_mine = sum_over_col(
        lambda zz: dot(mix, wo[:, pl.ds(pl.multiple_of(zz * 256, 256), 256)]),
        hid[...].astype(F32), set1, "proj").astype(BF16)
    att[col] = att_mine

    def a_copy(slot, dest):
        return rcopy(att.at[slot], att.at[slot], at_ss, at_rs.at[slot], dest)

    for off in FAR_FIRST:
        a_copy(col, rem(z + off, nz) * 2 + ylo).start()
    a_copy(col, ynb).start()
    for c in own_loads:
        c.wait()
    at_point("gather")
    ff = gv.shape[1]
    gate = jnp.zeros((128, ff), F32)
    up = jnp.zeros((128, ff), F32)
    sq = jnp.zeros((128, 128), F32)
    order = (0,) + NEAR_FIRST
    for k in range(nz + LAG):
        if 0 < k < nz:
            slot = rem(z + order[k], nz) * 2 + ylo
            a_copy(slot, ynb).wait_recv()
            a_copy(slot, ynb).start()
        if k >= LAG:
            at_point(f"block{k - LAG}")
            zz = rem(z + order[k - LAG], nz)
            a_copy(zz * 2 + 1 - ylo, ynb).wait_recv()
            pltpu.make_async_copy(
                att.at[zz * 2], att_o.at[:, pl.ds(pl.multiple_of(zz * 256, 256), 128)], out_sem.at[0]).start()
            pltpu.make_async_copy(
                att.at[zz * 2 + 1], att_o.at[:, pl.ds(pl.multiple_of(zz * 256 + 128, 128), 128)],
                out_sem.at[0]).start()
            n = jnp.concatenate([att[zz * 2], att[zz * 2 + 1]], axis=1)
            gate = gate + dot_nt(n, jnp.concatenate([gv[zz * 2], gv[zz * 2 + 1]], axis=1))
            up = up + dot_nt(n, jnp.concatenate([uv[zz * 2], uv[zz * 2 + 1]], axis=1))
            wide = n.astype(F32)
            wide = wide * wide
            sq = sq + wide[:, :128] + wide[:, 128:]
    scale = lax.rsqrt(jnp.sum(sq, axis=1, keepdims=True) * (1.0 / (128 * ncol)) + 1e-06)
    gate, up = gate * scale, up * scale
    act[...] = (gate / (1.0 + jnp.exp(-gate)) * up).astype(BF16)

    at_point("down")
    blk[...] = sum_over_col(
        lambda zz: dot(act[...], jnp.concatenate([dv[zz * 2], dv[zz * 2 + 1]], axis=1)),
        att_mine.astype(F32), set2, "down").astype(BF16)
    blk_out = pltpu.make_async_copy(blk, blk_o, out_sem.at[1])
    blk_out.start()

    for t in range(3):
        wgroup(t, 15).wait_send()
    q_all = q2.at[:, pl.ds(128, 128), :]
    pltpu.make_async_remote_copy(
        src_ref=q_all, dst_ref=q_all, send_sem=qs_sem, recv_sem=qr_sem.at[0],
        device_id=(sib, col), device_id_type=MESH).wait_send()
    for c in o_group(1, 2 * steps):
        c.wait_send()

    @pl.when(mine)
    def _():
        for c in o_group(0, 2 * steps - 1):
            c.wait_send()

    @pl.when(jnp.logical_not(mine))
    def _():
        for c in o_group(0, 2 * steps):
            c.wait_send()

    for ys, _yr, yss, yrs, zs, _zr, zss, zrs in (set1, set2):
        rcopy(ys, ys, yss, yrs.at[0], ynb).wait_send()
        most = zs.at[pl.ds(0, nz - 1)]
        rcopy(most, most, zss, zrs.at[0], ynb).wait_send()
    most = att.at[pl.ds(0, ncol - 1)]
    rcopy(most, most, at_ss, at_rs.at[0], ynb).wait_send()
    pltpu.make_async_copy(att_o, att_o, out_sem.at[0]).wait()
    blk_out.wait()


def write_out(a_h, b_h, a_o, b_o, a_v, b_v, sem):
    parts = 4
    size = a_v.shape[0] // parts

    def rows(ref, i):
        return ref.at[pl.ds(i * size, size), :]

    pieces = [(rows(a_h, i), rows(a_v, i), rows(a_o, i)) for i in range(parts)] + [(b_h, b_v, b_o)]
    ins = [pltpu.make_async_copy(h, v, sem.at[0, i]) for i, (h, v, o) in enumerate(pieces)]
    outs = [pltpu.make_async_copy(v, o, sem.at[1, i]) for i, (h, v, o) in enumerate(pieces)]
    for c in ins:
        c.start()
    for c, o in zip(ins, outs):
        c.wait()
        o.start()
    for o in outs:
        o.wait()


def solution(mesh):
    ncol, nrow = mesh.shape["col"], mesh.shape["row"]
    nx = nrow // 4
    placed = (
        P("row", None), P("col", None, None), P("col"), P("col"), P(), P("row", None), P(),
        P("col", None), P("row", "col"), P("row", "col"), P("col", "row"),
    )

    def on_device(queries, pool, table, plen, off, hidden, lup, wo, gate, up, down):
        rows, d = hidden.shape
        gate, up = gate.T, up.T
        ff = gate.shape[0]
        nkeys = pool.shape[0] * pool.shape[1]
        dma, vm = pltpu.SemaphoreType.DMA, pltpu.VMEM
        anyspec = pl.BlockSpec(memory_space=pl.ANY)
        smem = pl.BlockSpec(memory_space=pltpu.SMEM)
        blocks, half = (ncol, rows, 128), (ncol // 2, rows, 128)
        steps = H // 4
        two = 2 * rows
        scratch = [
            vm(pool.shape, BF16), vm((steps, LATENT, 512), BF16), vm((steps, two, 2 * QK), BF16),
            vm((rows, 128), BF16), vm(wo.shape, BF16),
            vm((nrow,) + gate.shape, BF16), vm((nrow,) + up.shape, BF16), vm((nrow,) + down.shape, BF16),
            vm((steps, 2, nkeys, 256), BF16), vm((steps, 2, nkeys, VDIM), BF16),
            vm((two, nkeys), F32), vm((two, nkeys), F32), vm((two, nkeys), BF16), vm((two, nkeys), BF16),
            vm((1, nkeys), jnp.int32), vm((two, nkeys), F32),
            vm((2, two, 128), F32), vm((2, two, 128), F32),
            vm((2,) + blocks, BF16), vm(blocks, BF16), vm((2, ncol, 8, 128), F32), vm((ncol, 8, 128), F32),
            vm(half, F32), vm(half, BF16), vm(half, BF16), vm(half, BF16), vm(half, BF16),
            vm(blocks, BF16), vm(half, BF16), vm(half, BF16), vm(half, BF16), vm(half, BF16),
            vm((rows, ff), BF16), vm((rows, 128), BF16),
            dma((3,)), dma((steps,)), dma((steps,)), dma((3,)), dma((2,)), dma((3,)), dma((3, nrow)), dma((3,)),
            dma, dma((steps,)), dma((2,)), dma, dma((2,)), dma,
            dma, dma((ncol // 2,)), dma, dma((ncol // 2,)), dma, dma((ncol,)),
            dma, dma((ncol // 2,)), dma, dma((ncol // 2,)),
        ]
        att, blk = pl.pallas_call(
            functools.partial(kernel, ncol, nx),
            out_shape=(
                jax.ShapeDtypeStruct((rows, d), BF16),
                jax.ShapeDtypeStruct((rows, d // ncol), BF16),
            ),
            in_specs=[anyspec, anyspec, smem, smem, smem] + [anyspec] * 6,
            out_specs=(anyspec, anyspec),
            scratch_shapes=scratch,
            compiler_params=pltpu.CompilerParams(
                collective_id=0, has_side_effects=True, vmem_limit_bytes=60 << 20),
            name="block",
        )(queries, pool, table, plen, off, hidden, lup, wo, gate, up, down)
        return pl.pallas_call(
            write_out,
            out_shape=(
                jax.ShapeDtypeStruct(att.shape, BF16),
                jax.ShapeDtypeStruct(blk.shape, BF16),
            ),
            in_specs=[anyspec] * 2,
            out_specs=(anyspec, anyspec),
            scratch_shapes=[vm(att.shape, BF16), vm(blk.shape, BF16), dma((2, 5))],
            name="write_out",
        )(att, blk)

    return jax.shard_map(
        on_device, mesh=mesh, in_specs=placed,
        out_specs=(P("row", None), P("row", "col")), check_vma=False,
    )
```

```python
import functools
import math

import jax
import jax.numpy as jnp
from jax import lax
from jax.experimental import pallas as pl
from jax.experimental.pallas import tpu as pltpu
from jax.sharding import PartitionSpec as P

H = 16
NOPE = 128
ROPE = 64
VDIM = 128
LATENT = 512
QK = 192
MESH = pl.DeviceIdType.MESH
LOW = -1e30
FAR = 1 << 30
SCALE2 = math.log2(math.e) / math.sqrt(QK)
F32 = jnp.float32
BF16 = jnp.bfloat16
YP, XP, XM, SIB, DN = range(5)
KEY_CHUNK = 256
EXPAND = 512
LAG = 3
ROWS = 16
BEFORE = 2
FAR_FIRST = (4, 3, 5, 2, 6, 1, 7)
NEAR_FIRST = (1, 7, 2, 6, 3, 5, 4)


def dot(a, b):
    return jnp.dot(a, b, preferred_element_type=F32)


def dot_nt(a, b):
    return lax.dot_general(a, b, (((1,), (1,)), ((), ())), preferred_element_type=F32)


def kernel(
    ncol, nx,
    q_h, pool_h, table_s, plen_s, off_s, hid_h, lup_h, wo_h, g_h, u_h, d_h,
    att_o, blk_o,
    lat, lupv, q2, hid, wo, gv, uv, dv, keys_all, vals_all, sc0, sc1, pr0, pr1, kpos, bias, bst, mx,
    o_send, o_recv, st_send, st_recv, own_term, y1_send, y1_recv, z1_send, z1_recv, att,
    y2_send, y2_recv, z2_send, z2_recv, act, blk,
    lsem, lup_sem, q_sem, own_sem, out_sem, ws_sem, wr_sem, wsib_sem, qs_sem, qr_sem,
    o_ss, o_rs, st_ss, st_rs, y1_ss, y1_rs, z1_ss, z1_rs, at_ss, at_rs, y2_ss, y2_rs, z2_ss, z2_rs,
):
    row, col = lax.axis_index("row"), lax.axis_index("col")

    def rem(a, b):
        return a % b

    def div(a, b):
        return a // b

    core, x, yhi = rem(row, 2), rem(div(row, 2), nx), div(row, 2 * nx)

    def row_of(yy, xx, cc):
        return (yy * nx + xx) * 2 + cc

    xp, xm, x2 = rem(x + 1, nx), rem(x + nx - 1, nx), rem(x + 2, nx)
    yo, co = 1 - yhi, 1 - core
    plus = [xp, xm, jnp.where(core == 0, xp, xm)]
    minus = [xm, xp, jnp.where(core == 0, xm, xp)]
    peers = [row_of(yo, x, core), row_of(yhi, xp, core), row_of(yhi, xm, core), row_of(yhi, x, co)]
    ups = [[row_of(yy, minus[t], core) for t in range(3)] for yy in (yhi, yo)]
    dns = [[row_of(yy, plus[t], core) for t in range(3)] for yy in (yhi, yo)]
    x2s = [row_of(yy, x2, core) for yy in (yhi, yo)]
    full = [gv, uv, dv]
    mine_h = [g_h, u_h, d_h]

    nz = ncol // 2
    z, ylo = div(col, 2), rem(col, 2)
    ynb = z * 2 + 1 - ylo
    sib = peers[SIB]
    steps = nz // 2
    turn = rem(core + z, 2)
    pair_at = [rem(z + 2 + 2 * i + turn, nz) for i in range(steps)]
    other_at = [rem(z + 2 + 2 * i + 1 - turn, nz) for i in range(steps)]

    loads = [
        pltpu.make_async_copy(pool_h, lat, lsem.at[0]),
        pltpu.make_async_copy(wo_h, wo, lsem.at[1]),
        pltpu.make_async_copy(hid_h.at[:, pl.ds(pl.multiple_of(col * 128, 128), 128)], hid, lsem.at[2]),
    ]

    def q_cols(p):
        return q_h.at[:, pl.ds(pl.multiple_of(p * 2 * QK, 2 * QK), 2 * QK)]

    lup_loads = [
        pltpu.make_async_copy(
            lup_h.at[:, pl.ds(pl.multiple_of(pair_at[i] * 512, 512), 512)], lupv.at[i], lup_sem.at[i])
        for i in range(steps)
    ]
    q_loads = [
        pltpu.make_async_copy(q_cols(pair_at[i]), q2.at[i, pl.ds(0, 128), :], q_sem.at[i])
        for i in range(steps)
    ]
    q_sends = [
        pltpu.make_async_remote_copy(
            src_ref=q_cols(other_at[i]), dst_ref=q2.at[i, pl.ds(128, 128), :],
            send_sem=qs_sem, recv_sem=qr_sem.at[i], device_id=(sib, col), device_id_type=MESH)
        for i in range(steps)
    ]
    lup_loads[0].start()
    loads[0].start()

    barrier = pltpu.get_barrier_semaphore()

    @pl.loop(1, ncol)
    def _(t):
        pl.semaphore_signal(barrier, inc=1, device_id=(row, rem(col + t, ncol)), device_id_type=MESH)

    @pl.loop(0, ncol)
    def _(t):
        pl.semaphore_signal(barrier, inc=1, device_id=(sib, rem(col + t, ncol)), device_id_type=MESH)

    for peer in peers[:SIB]:
        pl.semaphore_signal(barrier, inc=1, device_id=(peer, col), device_id_type=MESH)

    for c in q_loads + lup_loads[1:]:
        c.start()
    own_loads = [pltpu.make_async_copy(mine_h[t], full[t].at[row], own_sem.at[t]) for t in range(3)]
    for c in loads[1:] + own_loads:
        c.start()

    base = col * kpos.shape[1]
    lane = lax.broadcasted_iota(jnp.int32, kpos.shape, 1)
    page, slot = lax.shift_right_logical(lane, 6), lane & 63
    kp = jnp.full(kpos.shape, FAR, jnp.int32)
    for p in range(lat.shape[0]):
        here = jnp.where(slot < plen_s[p], base + p * 64 + slot, FAR)
        kp = jnp.where(page == table_s[p], here, kp)
    kpos[...] = kp
    sub = lax.broadcasted_iota(jnp.int32, (256, 1), 0)
    qpos = off_s[0] + jnp.where(sub < 128, row * 128 + sub, sib * 128 + sub - 128)

    nkeys = keys_all.shape[2]

    def make_bias():
        for rb in range(0, 256, 16):
            seen = kpos[...] <= qpos[rb:rb + 16]
            bias[rb:rb + 16, :] = jnp.where(seen, 0.0, LOW)

    bufs = [(keys_all.at[i], vals_all.at[i]) for i in range(steps)]

    def expand(i, kc, size):
        keys, vals = bufs[i]
        rows = slice(kc * size, (kc + 1) * size)
        pages = slice(kc * size // 64, (kc + 1) * size // 64)
        e = dot(lat[pages, :, :LATENT].reshape(size, LATENT), lupv[i]).astype(BF16)
        keys[0, rows, :NOPE] = e[:, :128]
        vals[0, rows, :] = e[:, 128:256]
        keys[1, rows, :NOPE] = e[:, 256:384]
        vals[1, rows, :] = e[:, 384:]

    make_bias()
    loads[0].wait()
    zeros64 = jnp.zeros((nkeys, 64), BF16)
    rope = jnp.concatenate([lat[:, :, LATENT:].reshape(nkeys, ROPE), zeros64], axis=1)
    for keys, _v in bufs:
        for hh in range(2):
            keys[hh, :, NOPE:] = rope


    def expand_pairs(first, last):
        for i in range(first, last):
            lup_loads[i].wait()
            for kc in range(nkeys // EXPAND):
                expand(i, kc, EXPAND)

    expand_pairs(0, BEFORE)

    pl.semaphore_wait(barrier, 2 * ncol - 1 + len(peers) - 1)
    for c in q_sends:
        c.start()

    def wcopy(t, owner, kind, dest, source=None):
        return pltpu.make_async_remote_copy(
            src_ref=full[t].at[owner] if source is None else source,
            dst_ref=full[t].at[owner],
            send_sem=ws_sem.at[t],
            recv_sem=wsib_sem.at[t] if kind == SIB else wr_sem.at[t, owner],
            device_id=(dest, col),
            device_id_type=MESH,
        )

    def wgroup(t, count):
        group = full[t].at[pl.ds(0, count)]
        return pltpu.make_async_remote_copy(
            src_ref=group, dst_ref=group, send_sem=ws_sem.at[t], recv_sem=wsib_sem.at[t],
            device_id=(sib, col), device_id_type=MESH)

    def wsend(t, owner, kind, dest, source=None):
        wcopy(t, owner, kind, dest, source).start()

    def warrive(t, owner):
        wcopy(t, owner, DN, sib).wait_recv()

    def stage_own(t):
        for kind in range(4):
            wsend(t, row, kind, peers[kind], mine_h[t])

    def stage_y(t):
        o = peers[YP]
        warrive(t, o)
        for kind in (XP, XM, SIB):
            wsend(t, o, kind, peers[kind])

    def stage_x(t, yy):
        up, dn = ups[yy][t], dns[yy][t]
        warrive(t, up)
        wsend(t, up, DN, dns[0][t])
        wsend(t, up, SIB, sib)
        warrive(t, dn)
        wsend(t, dn, SIB, sib)

    def stage_x2(t, yy):
        o = x2s[yy]
        warrive(t, o)
        wsend(t, o, SIB, sib)

    def stage_sib(t):
        wgroup(t, 2 * nx).wait_recv()

    plan = {
        "start": [(stage_own, 0), (stage_own, 1), (stage_own, 2)],
        3: [(stage_x, 0, 0), (stage_x, 1, 0), (stage_y, 0), (stage_y, 1)],
        "proj_y": [(stage_x, 2, 0), (stage_y, 2)],
        "proj_z": [(stage_x, 0, 1), (stage_x, 1, 1)],
        "gather": [(stage_x2, 0, 0), (stage_x2, 1, 0), (stage_x2, 0, 1), (stage_x2, 1, 1),
                   (stage_x, 2, 1), (stage_sib, 0), (stage_sib, 1)],
        "down": [(stage_x2, 2, 0), (stage_x2, 2, 1), (stage_sib, 2)],
    }

    def at_point(name):
        for stage, *which in plan.get(name, ()):
            stage(*which)

    at_point("start")

    expand_pairs(BEFORE, steps)

    def o_copies(part, head):
        dest = sib if part else row
        return (
            pltpu.make_async_remote_copy(
                src_ref=o_send.at[part, head], dst_ref=o_recv.at[col], send_sem=o_ss.at[part],
                recv_sem=o_rs, device_id=(dest, head), device_id_type=MESH),
            pltpu.make_async_remote_copy(
                src_ref=st_send.at[part, head], dst_ref=st_recv.at[col], send_sem=st_ss.at[part],
                recv_sem=st_rs, device_id=(dest, head), device_id_type=MESH),
        )

    lane128 = lax.broadcasted_iota(jnp.int32, (128, 128), 1)
    scs, prs = [sc0, sc1], [pr0, pr1]
    nchunk = nkeys // KEY_CHUNK
    mine = rem(div(col, 2) + core, 2) == 0
    for i in range(steps):
        q_loads[i].wait()
        q_sends[i].wait_recv()
    zq = jnp.zeros((256, 64), BF16)
    ones = jnp.ones((nkeys, 128), BF16)

    def score(n, kc):
        i, hh = n // 2, n % 2
        q = jnp.concatenate([q2[i, :, hh * QK:(hh + 1) * QK], zq], axis=1)
        ks = slice(kc * KEY_CHUNK, (kc + 1) * KEY_CHUNK)
        t = dot_nt(q, bufs[i][0][hh, ks, :]) * SCALE2 + bias[:, ks]
        scs[hh][:, ks] = t
        best = t[:, :128]
        for c in range(1, KEY_CHUNK // 128):
            best = jnp.maximum(best, t[:, c * 128:(c + 1) * 128])
        bst[hh] = best if kc == 0 else jnp.maximum(best, bst[hh])

    def soft(hh, rb):
        rows = slice(rb * ROWS, (rb + 1) * ROWS)
        m = mx[hh, rows, :]
        for c in range(nkeys // 128):
            ks = slice(c * 128, (c + 1) * 128)
            prs[hh][rows, ks] = jnp.exp2(scs[hh][rows, ks] - m).astype(BF16)

    for kc in range(nchunk):
        score(0, kc)
    for i in range(steps):
        for hh in range(2):
            n = 2 * i + hh
            m = jnp.max(bst[hh], axis=1, keepdims=True)
            mx[hh] = jnp.broadcast_to(jnp.where(m < 0.01 * LOW, 0.0, m), mx.shape[1:])
            for kc in range(nchunk):
                for rb in range(256 // ROWS // nchunk):
                    soft(hh, kc * (256 // ROWS // nchunk) + rb)
                if n + 1 < 2 * steps:
                    score(n + 1, kc)
            out = dot(prs[hh][...], jnp.concatenate([bufs[i][1][hh], ones], axis=1))
            head = pair_at[i] * 2 + hh
            for part in range(2):
                rs = slice(part * 128, (part + 1) * 128)
                total = out[rs, 128:]
                top = jnp.where(total > 0.0, mx[hh, rs, :], LOW)
                stats = jnp.where(lane128 == 0, top, jnp.where(lane128 == 1, total, 0.0))
                o_send[part, head] = out[rs, :128].astype(BF16)
                st_send[part, head] = stats.T[:8, :]
        for hh in range(2):
            head = pair_at[i] * 2 + hh
            for c in o_copies(1, head):
                c.start()

            @pl.when(head != col)
            def _():
                for c in o_copies(0, head):
                    c.start()

            @pl.when(head == col)
            def _():
                o_recv[col] = o_send[0, col]
                st_recv[col] = st_send[0, col]

        at_point(i)

    def o_group(part, count):
        o, st = o_recv.at[pl.ds(0, count)], st_recv.at[pl.ds(0, count)]
        return (
            pltpu.make_async_remote_copy(
                src_ref=o, dst_ref=o, send_sem=o_ss.at[part], recv_sem=o_rs,
                device_id=(sib, col), device_id_type=MESH),
            pltpu.make_async_remote_copy(
                src_ref=st, dst_ref=st, send_sem=st_ss.at[part], recv_sem=st_rs,
                device_id=(sib, col), device_id_type=MESH),
        )

    @pl.when(mine)
    def _():
        for c in o_group(0, ncol - 1):
            c.wait_recv()

    @pl.when(jnp.logical_not(mine))
    def _():
        for c in o_group(0, ncol):
            c.wait_recv()

    ms, ls = st_recv[:, 0, :], st_recv[:, 1, :]
    top = jnp.max(ms, axis=0, keepdims=True)
    wgt = jnp.exp2(ms - top)
    share = wgt / jnp.sum(wgt * ls, axis=0, keepdims=True)
    share = jnp.concatenate([share, jnp.zeros((128 - ncol, 128), F32)], axis=0).T
    mix = jnp.zeros((128, 128), F32)
    for s in range(ncol):
        mix = mix + share[:, s:s + 1] * o_recv[s].astype(F32)
    mix = mix.astype(BF16)

    def rcopy(src, dst, ss, rs, dest):
        return pltpu.make_async_remote_copy(
            src_ref=src, dst_ref=dst, send_sem=ss, recv_sem=rs, device_id=(row, dest), device_id_type=MESH)

    def y_copy(bufs5, zz):
        ys, yr, yss, yrs = bufs5[:4]
        return rcopy(ys.at[zz], yr.at[zz], yss, yrs.at[zz], ynb)

    def z_copy(bufs5, zz, mine_slot):
        zs, zr, zss, zrs = bufs5[4:]
        return rcopy(zs.at[zz], zr.at[mine_slot], zss, zrs.at[mine_slot], zz * 2 + ylo)

    def sum_over_col(term_of, start, bufs5, name):
        for off in FAR_FIRST + (0,):
            zz = rem(z + off, nz)
            both = term_of(zz)
            a, b = both[:, :128], both[:, 128:]
            own_term[zz] = jnp.where(ylo == 0, a, b)
            bufs5[0][zz] = jnp.where(ylo == 0, b, a).astype(BF16)
            y_copy(bufs5, zz).start()
        at_point(name + "_y")
        acc = start
        for off in FAR_FIRST + (0,):
            zz = rem(z + off, nz)
            y_copy(bufs5, zz).wait_recv()
            pair = own_term[zz] + bufs5[1][zz].astype(F32)
            if off:
                bufs5[4][zz] = pair.astype(BF16)
                z_copy(bufs5, zz, z).start()
            else:
                acc = acc + pair
        at_point(name + "_z")
        for off in NEAR_FIRST:
            zz = rem(z + off, nz)
            z_copy(bufs5, zz, zz).wait_recv()
            acc = acc + bufs5[5][zz].astype(F32)
        return acc

    set1 = (y1_send, y1_recv, y1_ss, y1_rs, z1_send, z1_recv, z1_ss, z1_rs)
    set2 = (y2_send, y2_recv, y2_ss, y2_rs, z2_send, z2_recv, z2_ss, z2_rs)

    loads[1].wait()
    loads[2].wait()
    att_mine = sum_over_col(
        lambda zz: dot(mix, wo[:, pl.ds(pl.multiple_of(zz * 256, 256), 256)]),
        hid[...].astype(F32), set1, "proj").astype(BF16)
    att[col] = att_mine

    def a_copy(slot, dest):
        return rcopy(att.at[slot], att.at[slot], at_ss, at_rs.at[slot], dest)

    for off in FAR_FIRST:
        a_copy(col, rem(z + off, nz) * 2 + ylo).start()
    a_copy(col, ynb).start()
    for c in own_loads:
        c.wait()
    at_point("gather")
    ff = gv.shape[1]
    gate = jnp.zeros((128, ff), F32)
    up = jnp.zeros((128, ff), F32)
    sq = jnp.zeros((128, 128), F32)
    order = (0,) + NEAR_FIRST
    for k in range(nz + LAG):
        if 0 < k < nz:
            slot = rem(z + order[k], nz) * 2 + ylo
            a_copy(slot, ynb).wait_recv()
            a_copy(slot, ynb).start()
        if k >= LAG:
            zz = rem(z + order[k - LAG], nz)
            a_copy(zz * 2 + 1 - ylo, ynb).wait_recv()
            pltpu.make_async_copy(
                att.at[zz * 2], att_o.at[:, pl.ds(pl.multiple_of(zz * 256, 256), 128)], out_sem.at[0]).start()
            pltpu.make_async_copy(
                att.at[zz * 2 + 1], att_o.at[:, pl.ds(pl.multiple_of(zz * 256 + 128, 128), 128)],
                out_sem.at[0]).start()
            n = jnp.concatenate([att[zz * 2], att[zz * 2 + 1]], axis=1)
            gate = gate + dot_nt(n, jnp.concatenate([gv[zz * 2], gv[zz * 2 + 1]], axis=1))
            up = up + dot_nt(n, jnp.concatenate([uv[zz * 2], uv[zz * 2 + 1]], axis=1))
            wide = n.astype(F32)
            wide = wide * wide
            sq = sq + wide[:, :128] + wide[:, 128:]
    scale = lax.rsqrt(jnp.sum(sq, axis=1, keepdims=True) * (1.0 / (128 * ncol)) + 1e-06)
    gate, up = gate * scale, up * scale
    act[...] = (gate / (1.0 + jnp.exp(-gate)) * up).astype(BF16)

    at_point("down")
    blk[...] = sum_over_col(
        lambda zz: dot(act[...], jnp.concatenate([dv[zz * 2], dv[zz * 2 + 1]], axis=1)),
        att_mine.astype(F32), set2, "down").astype(BF16)
    blk_out = pltpu.make_async_copy(blk, blk_o, out_sem.at[1])
    blk_out.start()

    for t in range(3):
        wgroup(t, 15).wait_send()
    q_all = q2.at[:, pl.ds(128, 128), :]
    pltpu.make_async_remote_copy(
        src_ref=q_all, dst_ref=q_all, send_sem=qs_sem, recv_sem=qr_sem.at[0],
        device_id=(sib, col), device_id_type=MESH).wait_send()
    for c in o_group(1, 2 * steps):
        c.wait_send()

    @pl.when(mine)
    def _():
        for c in o_group(0, 2 * steps - 1):
            c.wait_send()

    @pl.when(jnp.logical_not(mine))
    def _():
        for c in o_group(0, 2 * steps):
            c.wait_send()

    for ys, _yr, yss, yrs, zs, _zr, zss, zrs in (set1, set2):
        rcopy(ys, ys, yss, yrs.at[0], ynb).wait_send()
        most = zs.at[pl.ds(0, nz - 1)]
        rcopy(most, most, zss, zrs.at[0], ynb).wait_send()
    most = att.at[pl.ds(0, ncol - 1)]
    rcopy(most, most, at_ss, at_rs.at[0], ynb).wait_send()
    pltpu.make_async_copy(att_o, att_o, out_sem.at[0]).wait()
    blk_out.wait()


def write_out(a_h, b_h, a_o, b_o, a_v, b_v, sem):
    parts = 4
    size = a_v.shape[0] // parts

    def rows(ref, i):
        return ref.at[pl.ds(i * size, size), :]

    pieces = [(rows(a_h, i), rows(a_v, i), rows(a_o, i)) for i in range(parts)] + [(b_h, b_v, b_o)]
    ins = [pltpu.make_async_copy(h, v, sem.at[0, i]) for i, (h, v, o) in enumerate(pieces)]
    outs = [pltpu.make_async_copy(v, o, sem.at[1, i]) for i, (h, v, o) in enumerate(pieces)]
    for c in ins:
        c.start()
    for c, o in zip(ins, outs):
        c.wait()
        o.start()
    for o in outs:
        o.wait()


def solution(mesh):
    ncol, nrow = mesh.shape["col"], mesh.shape["row"]
    nx = nrow // 4
    placed = (
        P("row", None), P("col", None, None), P("col"), P("col"), P(), P("row", None), P(),
        P("col", None), P("row", "col"), P("row", "col"), P("col", "row"),
    )

    def on_device(queries, pool, table, plen, off, hidden, lup, wo, gate, up, down):
        rows, d = hidden.shape
        gate, up = gate.T, up.T
        ff = gate.shape[0]
        nkeys = pool.shape[0] * pool.shape[1]
        dma, vm = pltpu.SemaphoreType.DMA, pltpu.VMEM
        anyspec = pl.BlockSpec(memory_space=pl.ANY)
        smem = pl.BlockSpec(memory_space=pltpu.SMEM)
        blocks, half = (ncol, rows, 128), (ncol // 2, rows, 128)
        steps = H // 4
        two = 2 * rows
        scratch = [
            vm(pool.shape, BF16), vm((steps, LATENT, 512), BF16), vm((steps, two, 2 * QK), BF16),
            vm((rows, 128), BF16), vm(wo.shape, BF16),
            vm((nrow,) + gate.shape, BF16), vm((nrow,) + up.shape, BF16), vm((nrow,) + down.shape, BF16),
            vm((steps, 2, nkeys, 256), BF16), vm((steps, 2, nkeys, VDIM), BF16),
            vm((two, nkeys), F32), vm((two, nkeys), F32), vm((two, nkeys), BF16), vm((two, nkeys), BF16),
            vm((1, nkeys), jnp.int32), vm((two, nkeys), F32),
            vm((2, two, 128), F32), vm((2, two, 128), F32),
            vm((2,) + blocks, BF16), vm(blocks, BF16), vm((2, ncol, 8, 128), F32), vm((ncol, 8, 128), F32),
            vm(half, F32), vm(half, BF16), vm(half, BF16), vm(half, BF16), vm(half, BF16),
            vm(blocks, BF16), vm(half, BF16), vm(half, BF16), vm(half, BF16), vm(half, BF16),
            vm((rows, ff), BF16), vm((rows, 128), BF16),
            dma((3,)), dma((steps,)), dma((steps,)), dma((3,)), dma((2,)), dma((3,)), dma((3, nrow)), dma((3,)),
            dma, dma((steps,)), dma((2,)), dma, dma((2,)), dma,
            dma, dma((ncol // 2,)), dma, dma((ncol // 2,)), dma, dma((ncol,)),
            dma, dma((ncol // 2,)), dma, dma((ncol // 2,)),
        ]
        att, blk = pl.pallas_call(
            functools.partial(kernel, ncol, nx),
            out_shape=(
                jax.ShapeDtypeStruct((rows, d), BF16),
                jax.ShapeDtypeStruct((rows, d // ncol), BF16),
            ),
            in_specs=[anyspec, anyspec, smem, smem, smem] + [anyspec] * 6,
            out_specs=(anyspec, anyspec),
            scratch_shapes=scratch,
            compiler_params=pltpu.CompilerParams(
                collective_id=0, has_side_effects=True, vmem_limit_bytes=60 << 20),
            name="block",
        )(queries, pool, table, plen, off, hidden, lup, wo, gate, up, down)
        return pl.pallas_call(
            write_out,
            out_shape=(
                jax.ShapeDtypeStruct(att.shape, BF16),
                jax.ShapeDtypeStruct(blk.shape, BF16),
            ),
            in_specs=[anyspec] * 2,
            out_specs=(anyspec, anyspec),
            scratch_shapes=[vm(att.shape, BF16), vm(blk.shape, BF16), dma((2, 5))],
            name="write_out",
        )(att, blk)

    return jax.shard_map(
        on_device, mesh=mesh, in_specs=placed,
        out_specs=(P("row", None), P("row", "col")), check_vma=False,
    )
```

```python
import functools
import math

import jax
import jax.numpy as jnp
from jax import lax
from jax.experimental import pallas as pl
from jax.experimental.pallas import tpu as pltpu
from jax.sharding import PartitionSpec as P

H = 16
NOPE = 128
ROPE = 64
VDIM = 128
LATENT = 512
QK = 192
MESH = pl.DeviceIdType.MESH
LOW = -1e30
FAR = 1 << 30
SCALE2 = math.log2(math.e) / math.sqrt(QK)
F32 = jnp.float32
BF16 = jnp.bfloat16
YP, XP, XM, SIB, DN = range(5)
KEY_CHUNK = 256
EXPAND = 512
LAG = 3
ROWS = 16
BEFORE = 2
FAR_FIRST = (4, 3, 5, 2, 6, 1, 7)
NEAR_FIRST = (1, 7, 2, 6, 3, 5, 4)


def dot(a, b):
    return jnp.dot(a, b, preferred_element_type=F32)


def dot_nt(a, b):
    return lax.dot_general(a, b, (((1,), (1,)), ((), ())), preferred_element_type=F32)


def kernel(
    ncol, nx,
    q_h, pool_h, table_s, plen_s, off_s, hid_h, lup_h, wo_h, g_h, u_h, d_h,
    att_o, blk_o,
    lat, lupv, q2, hid, wo, gv, uv, dv, keys_all, vals_all, sc0, sc1, pr0, pr1, kpos, bias, bst, mx,
    o_send, o_recv, st_send, st_recv, own_term, y1_send, y1_recv, z1_send, z1_recv, att,
    y2_send, y2_recv, z2_send, z2_recv, act, blk,
    lsem, lup_sem, q_sem, own_sem, out_sem, ws_sem, wr_sem, wsib_sem, qs_sem, qr_sem,
    o_ss, o_rs, st_ss, st_rs, y1_ss, y1_rs, z1_ss, z1_rs, at_ss, at_rs, y2_ss, y2_rs, z2_ss, z2_rs,
):
    row, col = lax.axis_index("row"), lax.axis_index("col")

    def rem(a, b):
        return a % b

    def div(a, b):
        return a // b

    core, x, yhi = rem(row, 2), rem(div(row, 2), nx), div(row, 2 * nx)

    def row_of(yy, xx, cc):
        return (yy * nx + xx) * 2 + cc

    xp, xm, x2 = rem(x + 1, nx), rem(x + nx - 1, nx), rem(x + 2, nx)
    yo, co = 1 - yhi, 1 - core
    plus = [xp, xm, jnp.where(core == 0, xp, xm)]
    minus = [xm, xp, jnp.where(core == 0, xm, xp)]
    peers = [row_of(yo, x, core), row_of(yhi, xp, core), row_of(yhi, xm, core), row_of(yhi, x, co)]
    ups = [[row_of(yy, minus[t], core) for t in range(3)] for yy in (yhi, yo)]
    dns = [[row_of(yy, plus[t], core) for t in range(3)] for yy in (yhi, yo)]
    x2s = [row_of(yy, x2, core) for yy in (yhi, yo)]
    full = [gv, uv, dv]
    mine_h = [g_h, u_h, d_h]

    nz = ncol // 2
    z, ylo = div(col, 2), rem(col, 2)
    ynb = z * 2 + 1 - ylo
    sib = peers[SIB]
    steps = nz // 2
    turn = rem(core + z, 2)
    pair_at = [rem(z + 2 + 2 * i + turn, nz) for i in range(steps)]
    other_at = [rem(z + 2 + 2 * i + 1 - turn, nz) for i in range(steps)]

    loads = [
        pltpu.make_async_copy(pool_h, lat, lsem.at[0]),
        pltpu.make_async_copy(wo_h, wo, lsem.at[1]),
        pltpu.make_async_copy(hid_h.at[:, pl.ds(pl.multiple_of(col * 128, 128), 128)], hid, lsem.at[2]),
    ]

    def q_cols(p):
        return q_h.at[:, pl.ds(pl.multiple_of(p * 2 * QK, 2 * QK), 2 * QK)]

    lup_loads = [
        pltpu.make_async_copy(
            lup_h.at[:, pl.ds(pl.multiple_of(pair_at[i] * 512, 512), 512)], lupv.at[i], lup_sem.at[i])
        for i in range(steps)
    ]
    q_loads = [
        pltpu.make_async_copy(q_cols(pair_at[i]), q2.at[i, pl.ds(0, 128), :], q_sem.at[i])
        for i in range(steps)
    ]
    q_sends = [
        pltpu.make_async_remote_copy(
            src_ref=q_cols(other_at[i]), dst_ref=q2.at[i, pl.ds(128, 128), :],
            send_sem=qs_sem, recv_sem=qr_sem.at[i], device_id=(sib, col), device_id_type=MESH)
        for i in range(steps)
    ]
    lup_loads[0].start()
    loads[0].start()

    barrier = pltpu.get_barrier_semaphore()

    @pl.loop(1, ncol)
    def _(t):
        pl.semaphore_signal(barrier, inc=1, device_id=(row, rem(col + t, ncol)), device_id_type=MESH)

    @pl.loop(0, ncol)
    def _(t):
        pl.semaphore_signal(barrier, inc=1, device_id=(sib, rem(col + t, ncol)), device_id_type=MESH)

    for peer in peers[:SIB]:
        pl.semaphore_signal(barrier, inc=1, device_id=(peer, col), device_id_type=MESH)

    for c in q_loads + lup_loads[1:]:
        c.start()
    own_loads = [pltpu.make_async_copy(mine_h[t], full[t].at[row], own_sem.at[t]) for t in range(3)]
    for c in loads[1:] + own_loads:
        c.start()

    base = col * kpos.shape[1]
    lane = lax.broadcasted_iota(jnp.int32, kpos.shape, 1)
    page, slot = lax.shift_right_logical(lane, 6), lane & 63
    kp = jnp.full(kpos.shape, FAR, jnp.int32)
    for p in range(lat.shape[0]):
        here = jnp.where(slot < plen_s[p], base + p * 64 + slot, FAR)
        kp = jnp.where(page == table_s[p], here, kp)
    kpos[...] = kp
    sub = lax.broadcasted_iota(jnp.int32, (256, 1), 0)
    qpos = off_s[0] + jnp.where(sub < 128, row * 128 + sub, sib * 128 + sub - 128)

    nkeys = keys_all.shape[2]

    def make_bias():
        for rb in range(0, 256, 16):
            seen = kpos[...] <= qpos[rb:rb + 16]
            bias[rb:rb + 16, :] = jnp.where(seen, 0.0, LOW)

    bufs = [(keys_all.at[i], vals_all.at[i]) for i in range(steps)]

    def expand(i, kc, size):
        keys, vals = bufs[i]
        rows = slice(kc * size, (kc + 1) * size)
        pages = slice(kc * size // 64, (kc + 1) * size // 64)
        e = dot(lat[pages, :, :LATENT].reshape(size, LATENT), lupv[i]).astype(BF16)
        keys[0, rows, :NOPE] = e[:, :128]
        vals[0, rows, :] = e[:, 128:256]
        keys[1, rows, :NOPE] = e[:, 256:384]
        vals[1, rows, :] = e[:, 384:]

    make_bias()
    loads[0].wait()
    zeros64 = jnp.zeros((nkeys, 64), BF16)
    rope = jnp.concatenate([lat[:, :, LATENT:].reshape(nkeys, ROPE), zeros64], axis=1)
    for keys, _v in bufs:
        for hh in range(2):
            keys[hh, :, NOPE:] = rope


    def expand_pairs(first, last):
        for i in range(first, last):
            lup_loads[i].wait()
            for kc in range(nkeys // EXPAND):
                expand(i, kc, EXPAND)

    expand_pairs(0, BEFORE)

    pl.semaphore_wait(barrier, 2 * ncol - 1 + len(peers) - 1)
    for c in q_sends:
        c.start()

    def wcopy(t, owner, kind, dest, source=None):
        return pltpu.make_async_remote_copy(
            src_ref=full[t].at[owner] if source is None else source,
            dst_ref=full[t].at[owner],
            send_sem=ws_sem.at[t],
            recv_sem=wsib_sem.at[t] if kind == SIB else wr_sem.at[t, owner],
            device_id=(dest, col),
            device_id_type=MESH,
        )

    def wgroup(t, count):
        group = full[t].at[pl.ds(0, count)]
        return pltpu.make_async_remote_copy(
            src_ref=group, dst_ref=group, send_sem=ws_sem.at[t], recv_sem=wsib_sem.at[t],
            device_id=(sib, col), device_id_type=MESH)

    def wsend(t, owner, kind, dest, source=None):
        wcopy(t, owner, kind, dest, source).start()

    def warrive(t, owner):
        wcopy(t, owner, DN, sib).wait_recv()

    def stage_own(t):
        for kind in range(4):
            wsend(t, row, kind, peers[kind], mine_h[t])

    def stage_y(t):
        o = peers[YP]
        warrive(t, o)
        for kind in (XP, XM, SIB):
            wsend(t, o, kind, peers[kind])

    def stage_x(t, yy):
        up, dn = ups[yy][t], dns[yy][t]
        warrive(t, up)
        wsend(t, up, DN, dns[0][t])
        wsend(t, up, SIB, sib)
        warrive(t, dn)
        wsend(t, dn, SIB, sib)

    def stage_x2(t, yy):
        o = x2s[yy]
        warrive(t, o)
        wsend(t, o, SIB, sib)

    def stage_sib(t):
        wgroup(t, 2 * nx).wait_recv()

    plan = {
        "start": [(stage_own, 0), (stage_own, 1), (stage_own, 2)],
        2: [(stage_x, 0, 0), (stage_x, 1, 0)],
        3: [(stage_y, 0), (stage_y, 1), (stage_x, 2, 0)],
        "proj_y": [(stage_y, 2)],
        "proj_z": [(stage_x, 0, 1), (stage_x, 1, 1)],
        "gather": [(stage_x2, 0, 0), (stage_x2, 1, 0), (stage_x, 2, 1), (stage_x2, 0, 1), (stage_x2, 1, 1),
                   (stage_sib, 0), (stage_sib, 1)],
        "down": [(stage_x2, 2, 0), (stage_x2, 2, 1), (stage_sib, 2)],
    }

    def at_point(name):
        for stage, *which in plan.get(name, ()):
            stage(*which)

    at_point("start")

    expand_pairs(BEFORE, steps)

    def o_copies(part, head):
        dest = sib if part else row
        return (
            pltpu.make_async_remote_copy(
                src_ref=o_send.at[part, head], dst_ref=o_recv.at[col], send_sem=o_ss.at[part],
                recv_sem=o_rs, device_id=(dest, head), device_id_type=MESH),
            pltpu.make_async_remote_copy(
                src_ref=st_send.at[part, head], dst_ref=st_recv.at[col], send_sem=st_ss.at[part],
                recv_sem=st_rs, device_id=(dest, head), device_id_type=MESH),
        )

    lane128 = lax.broadcasted_iota(jnp.int32, (128, 128), 1)
    scs, prs = [sc0, sc1], [pr0, pr1]
    nchunk = nkeys // KEY_CHUNK
    mine = rem(div(col, 2) + core, 2) == 0
    for i in range(steps):
        q_loads[i].wait()
        q_sends[i].wait_recv()
    zq = jnp.zeros((256, 64), BF16)
    ones = jnp.ones((nkeys, 128), BF16)

    def score(n, kc):
        i, hh = n // 2, n % 2
        q = jnp.concatenate([q2[i, :, hh * QK:(hh + 1) * QK], zq], axis=1)
        ks = slice(kc * KEY_CHUNK, (kc + 1) * KEY_CHUNK)
        t = dot_nt(q, bufs[i][0][hh, ks, :]) * SCALE2 + bias[:, ks]
        scs[hh][:, ks] = t
        best = t[:, :128]
        for c in range(1, KEY_CHUNK // 128):
            best = jnp.maximum(best, t[:, c * 128:(c + 1) * 128])
        bst[hh] = best if kc == 0 else jnp.maximum(best, bst[hh])

    def soft(hh, rb):
        rows = slice(rb * ROWS, (rb + 1) * ROWS)
        m = mx[hh, rows, :]
        for c in range(nkeys // 128):
            ks = slice(c * 128, (c + 1) * 128)
            prs[hh][rows, ks] = jnp.exp2(scs[hh][rows, ks] - m).astype(BF16)

    for kc in range(nchunk):
        score(0, kc)
    for i in range(steps):
        for hh in range(2):
            n = 2 * i + hh
            m = jnp.max(bst[hh], axis=1, keepdims=True)
            mx[hh] = jnp.broadcast_to(jnp.where(m < 0.01 * LOW, 0.0, m), mx.shape[1:])
            for kc in range(nchunk):
                for rb in range(256 // ROWS // nchunk):
                    soft(hh, kc * (256 // ROWS // nchunk) + rb)
                if n + 1 < 2 * steps:
                    score(n + 1, kc)
            out = dot(prs[hh][...], jnp.concatenate([bufs[i][1][hh], ones], axis=1))
            head = pair_at[i] * 2 + hh
            for part in range(2):
                rs = slice(part * 128, (part + 1) * 128)
                total = out[rs, 128:]
                top = jnp.where(total > 0.0, mx[hh, rs, :], LOW)
                stats = jnp.where(lane128 == 0, top, jnp.where(lane128 == 1, total, 0.0))
                o_send[part, head] = out[rs, :128].astype(BF16)
                st_send[part, head] = stats.T[:8, :]
        for hh in range(2):
            head = pair_at[i] * 2 + hh
            for c in o_copies(1, head):
                c.start()

            @pl.when(head != col)
            def _():
                for c in o_copies(0, head):
                    c.start()

            @pl.when(head == col)
            def _():
                o_recv[col] = o_send[0, col]
                st_recv[col] = st_send[0, col]

        at_point(i)

    def o_group(part, count):
        o, st = o_recv.at[pl.ds(0, count)], st_recv.at[pl.ds(0, count)]
        return (
            pltpu.make_async_remote_copy(
                src_ref=o, dst_ref=o, send_sem=o_ss.at[part], recv_sem=o_rs,
                device_id=(sib, col), device_id_type=MESH),
            pltpu.make_async_remote_copy(
                src_ref=st, dst_ref=st, send_sem=st_ss.at[part], recv_sem=st_rs,
                device_id=(sib, col), device_id_type=MESH),
        )

    @pl.when(mine)
    def _():
        for c in o_group(0, ncol - 1):
            c.wait_recv()

    @pl.when(jnp.logical_not(mine))
    def _():
        for c in o_group(0, ncol):
            c.wait_recv()

    ms, ls = st_recv[:, 0, :], st_recv[:, 1, :]
    top = jnp.max(ms, axis=0, keepdims=True)
    wgt = jnp.exp2(ms - top)
    share = wgt / jnp.sum(wgt * ls, axis=0, keepdims=True)
    share = jnp.concatenate([share, jnp.zeros((128 - ncol, 128), F32)], axis=0).T
    mix = jnp.zeros((128, 128), F32)
    for s in range(ncol):
        mix = mix + share[:, s:s + 1] * o_recv[s].astype(F32)
    mix = mix.astype(BF16)

    def rcopy(src, dst, ss, rs, dest):
        return pltpu.make_async_remote_copy(
            src_ref=src, dst_ref=dst, send_sem=ss, recv_sem=rs, device_id=(row, dest), device_id_type=MESH)

    def y_copy(bufs5, zz):
        ys, yr, yss, yrs = bufs5[:4]
        return rcopy(ys.at[zz], yr.at[zz], yss, yrs.at[zz], ynb)

    def z_copy(bufs5, zz, mine_slot):
        zs, zr, zss, zrs = bufs5[4:]
        return rcopy(zs.at[zz], zr.at[mine_slot], zss, zrs.at[mine_slot], zz * 2 + ylo)

    def sum_over_col(term_of, start, bufs5, name):
        for off in FAR_FIRST + (0,):
            zz = rem(z + off, nz)
            both = term_of(zz)
            a, b = both[:, :128], both[:, 128:]
            own_term[zz] = jnp.where(ylo == 0, a, b)
            bufs5[0][zz] = jnp.where(ylo == 0, b, a).astype(BF16)
            y_copy(bufs5, zz).start()
        at_point(name + "_y")
        acc = start
        for off in FAR_FIRST + (0,):
            zz = rem(z + off, nz)
            y_copy(bufs5, zz).wait_recv()
            pair = own_term[zz] + bufs5[1][zz].astype(F32)
            if off:
                bufs5[4][zz] = pair.astype(BF16)
                z_copy(bufs5, zz, z).start()
            else:
                acc = acc + pair
        at_point(name + "_z")
        for off in NEAR_FIRST:
            zz = rem(z + off, nz)
            z_copy(bufs5, zz, zz).wait_recv()
            acc = acc + bufs5[5][zz].astype(F32)
        return acc

    set1 = (y1_send, y1_recv, y1_ss, y1_rs, z1_send, z1_recv, z1_ss, z1_rs)
    set2 = (y2_send, y2_recv, y2_ss, y2_rs, z2_send, z2_recv, z2_ss, z2_rs)

    loads[1].wait()
    loads[2].wait()
    att_mine = sum_over_col(
        lambda zz: dot(mix, wo[:, pl.ds(pl.multiple_of(zz * 256, 256), 256)]),
        hid[...].astype(F32), set1, "proj").astype(BF16)
    att[col] = att_mine

    def a_copy(slot, dest):
        return rcopy(att.at[slot], att.at[slot], at_ss, at_rs.at[slot], dest)

    for off in FAR_FIRST:
        a_copy(col, rem(z + off, nz) * 2 + ylo).start()
    a_copy(col, ynb).start()
    for c in own_loads:
        c.wait()
    at_point("gather")
    ff = gv.shape[1]
    gate = jnp.zeros((128, ff), F32)
    up = jnp.zeros((128, ff), F32)
    sq = jnp.zeros((128, 128), F32)
    order = (0,) + NEAR_FIRST
    for k in range(nz + LAG):
        if 0 < k < nz:
            slot = rem(z + order[k], nz) * 2 + ylo
            a_copy(slot, ynb).wait_recv()
            a_copy(slot, ynb).start()
        if k >= LAG:
            zz = rem(z + order[k - LAG], nz)
            a_copy(zz * 2 + 1 - ylo, ynb).wait_recv()
            pltpu.make_async_copy(
                att.at[zz * 2], att_o.at[:, pl.ds(pl.multiple_of(zz * 256, 256), 128)], out_sem.at[0]).start()
            pltpu.make_async_copy(
                att.at[zz * 2 + 1], att_o.at[:, pl.ds(pl.multiple_of(zz * 256 + 128, 128), 128)],
                out_sem.at[0]).start()
            n = jnp.concatenate([att[zz * 2], att[zz * 2 + 1]], axis=1)
            gate = gate + dot_nt(n, jnp.concatenate([gv[zz * 2], gv[zz * 2 + 1]], axis=1))
            up = up + dot_nt(n, jnp.concatenate([uv[zz * 2], uv[zz * 2 + 1]], axis=1))
            wide = n.astype(F32)
            wide = wide * wide
            sq = sq + wide[:, :128] + wide[:, 128:]
    scale = lax.rsqrt(jnp.sum(sq, axis=1, keepdims=True) * (1.0 / (128 * ncol)) + 1e-06)
    gate, up = gate * scale, up * scale
    act[...] = (gate / (1.0 + jnp.exp(-gate)) * up).astype(BF16)

    at_point("down")
    blk[...] = sum_over_col(
        lambda zz: dot(act[...], jnp.concatenate([dv[zz * 2], dv[zz * 2 + 1]], axis=1)),
        att_mine.astype(F32), set2, "down").astype(BF16)
    blk_out = pltpu.make_async_copy(blk, blk_o, out_sem.at[1])
    blk_out.start()

    for t in range(3):
        wgroup(t, 15).wait_send()
    q_all = q2.at[:, pl.ds(128, 128), :]
    pltpu.make_async_remote_copy(
        src_ref=q_all, dst_ref=q_all, send_sem=qs_sem, recv_sem=qr_sem.at[0],
        device_id=(sib, col), device_id_type=MESH).wait_send()
    for c in o_group(1, 2 * steps):
        c.wait_send()

    @pl.when(mine)
    def _():
        for c in o_group(0, 2 * steps - 1):
            c.wait_send()

    @pl.when(jnp.logical_not(mine))
    def _():
        for c in o_group(0, 2 * steps):
            c.wait_send()

    for ys, _yr, yss, yrs, zs, _zr, zss, zrs in (set1, set2):
        rcopy(ys, ys, yss, yrs.at[0], ynb).wait_send()
        most = zs.at[pl.ds(0, nz - 1)]
        rcopy(most, most, zss, zrs.at[0], ynb).wait_send()
    most = att.at[pl.ds(0, ncol - 1)]
    rcopy(most, most, at_ss, at_rs.at[0], ynb).wait_send()
    pltpu.make_async_copy(att_o, att_o, out_sem.at[0]).wait()
    blk_out.wait()


def write_out(a_h, b_h, a_o, b_o, a_v, b_v, sem):
    parts = 4
    size = a_v.shape[0] // parts

    def rows(ref, i):
        return ref.at[pl.ds(i * size, size), :]

    pieces = [(rows(a_h, i), rows(a_v, i), rows(a_o, i)) for i in range(parts)] + [(b_h, b_v, b_o)]
    ins = [pltpu.make_async_copy(h, v, sem.at[0, i]) for i, (h, v, o) in enumerate(pieces)]
    outs = [pltpu.make_async_copy(v, o, sem.at[1, i]) for i, (h, v, o) in enumerate(pieces)]
    for c in ins:
        c.start()
    for c, o in zip(ins, outs):
        c.wait()
        o.start()
    for o in outs:
        o.wait()


def solution(mesh):
    ncol, nrow = mesh.shape["col"], mesh.shape["row"]
    nx = nrow // 4
    placed = (
        P("row", None), P("col", None, None), P("col"), P("col"), P(), P("row", None), P(),
        P("col", None), P("row", "col"), P("row", "col"), P("col", "row"),
    )

    def on_device(queries, pool, table, plen, off, hidden, lup, wo, gate, up, down):
        rows, d = hidden.shape
        gate, up = gate.T, up.T
        ff = gate.shape[0]
        nkeys = pool.shape[0] * pool.shape[1]
        dma, vm = pltpu.SemaphoreType.DMA, pltpu.VMEM
        anyspec = pl.BlockSpec(memory_space=pl.ANY)
        smem = pl.BlockSpec(memory_space=pltpu.SMEM)
        blocks, half = (ncol, rows, 128), (ncol // 2, rows, 128)
        steps = H // 4
        two = 2 * rows
        scratch = [
            vm(pool.shape, BF16), vm((steps, LATENT, 512), BF16), vm((steps, two, 2 * QK), BF16),
            vm((rows, 128), BF16), vm(wo.shape, BF16),
            vm((nrow,) + gate.shape, BF16), vm((nrow,) + up.shape, BF16), vm((nrow,) + down.shape, BF16),
            vm((steps, 2, nkeys, 256), BF16), vm((steps, 2, nkeys, VDIM), BF16),
            vm((two, nkeys), F32), vm((two, nkeys), F32), vm((two, nkeys), BF16), vm((two, nkeys), BF16),
            vm((1, nkeys), jnp.int32), vm((two, nkeys), F32),
            vm((2, two, 128), F32), vm((2, two, 128), F32),
            vm((2,) + blocks, BF16), vm(blocks, BF16), vm((2, ncol, 8, 128), F32), vm((ncol, 8, 128), F32),
            vm(half, F32), vm(half, BF16), vm(half, BF16), vm(half, BF16), vm(half, BF16),
            vm(blocks, BF16), vm(half, BF16), vm(half, BF16), vm(half, BF16), vm(half, BF16),
            vm((rows, ff), BF16), vm((rows, 128), BF16),
            dma((3,)), dma((steps,)), dma((steps,)), dma((3,)), dma((2,)), dma((3,)), dma((3, nrow)), dma((3,)),
            dma, dma((steps,)), dma((2,)), dma, dma((2,)), dma,
            dma, dma((ncol // 2,)), dma, dma((ncol // 2,)), dma, dma((ncol,)),
            dma, dma((ncol // 2,)), dma, dma((ncol // 2,)),
        ]
        att, blk = pl.pallas_call(
            functools.partial(kernel, ncol, nx),
            out_shape=(
                jax.ShapeDtypeStruct((rows, d), BF16),
                jax.ShapeDtypeStruct((rows, d // ncol), BF16),
            ),
            in_specs=[anyspec, anyspec, smem, smem, smem] + [anyspec] * 6,
            out_specs=(anyspec, anyspec),
            scratch_shapes=scratch,
            compiler_params=pltpu.CompilerParams(
                collective_id=0, has_side_effects=True, vmem_limit_bytes=60 << 20),
            name="block",
        )(queries, pool, table, plen, off, hidden, lup, wo, gate, up, down)
        return pl.pallas_call(
            write_out,
            out_shape=(
                jax.ShapeDtypeStruct(att.shape, BF16),
                jax.ShapeDtypeStruct(blk.shape, BF16),
            ),
            in_specs=[anyspec] * 2,
            out_specs=(anyspec, anyspec),
            scratch_shapes=[vm(att.shape, BF16), vm(blk.shape, BF16), dma((2, 5))],
            name="write_out",
        )(att, blk)

    return jax.shard_map(
        on_device, mesh=mesh, in_specs=placed,
        out_specs=(P("row", None), P("row", "col")), check_vma=False,
    )
```
